32 devices in a mesh: tm: 2 (over y), aux: 16 (over z, x, core).
Axes of the slice: x: 2, y: 2, z: 4, core: 2. Of those that a mesh axis runs over, the one named last changes fastest.
Arguments:
- green: bfloat16 [4, 1024, 1024], P('tm'), may hold values from -4 to 4
- factors: bfloat16 [4096, 1024], P('aux'), may hold values from -0.1875 to 0.1875
- pattern: int32 [32, 8], P('aux'), may hold values 0 or 1
- coulomb: float32 [4096], P('aux'), may hold values from 0.5 to 2
Outputs:
- sigma: float32 [1024, 4, 1024], P('aux', 'tm')
The draws below stay inside these ranges and needn't reach their ends.
All inputs are finite; a program needn't handle non-finite values. No bound on the sum of `pattern` on one device may be relied on, other than what follows from the above.
Results may differ from the reference program's by a relative error of at most 0.006.
Values may be sent and summed in bfloat16 or wider, within the bound.
A program may use at most 64 MiB of HBM per device.

```python
import math
import jax
import jax.numpy as jnp
from jax import lax

ORB = 1024
AUX = 4096
BLOCK = 128
TIMES = 4


def plant(result, own_key, smallest, top_value):
    dims = result.shape
    index_at = [jax.random.randint(jax.random.fold_in(own_key, axis), (), 0, dims[axis]) for axis in range(len(dims))]
    result = result.at[tuple(index_at)].set(smallest)
    longest = dims.index(max(dims))
    index_at[longest] = (index_at[longest] + 1) % dims[longest]
    return result.at[tuple(index_at)].set(top_value)


def block_levels(key, shape, shards, smallest, top_value):
    loudness, own = 1.0, jax.random.fold_in(key, 6)
    for axis_at, blocks in shards:
        heights = jnp.exp(jax.random.uniform(jax.random.fold_in(own, axis_at), (blocks,), jnp.float32, smallest / len(shards), top_value / len(shards)))
        loudness = loudness * jnp.repeat(heights, shape[axis_at] // blocks).reshape([-1 if axis == axis_at else 1 for axis in range(len(shape))])
    return loudness


def normal_values(rng, dims, spread, reach, pieces=(), kind=jnp.bfloat16):
    entries = jax.random.normal(rng, dims, jnp.float32) * spread
    if len(pieces) > 0:
        entries = block_levels(rng, dims, pieces, -0.22, 0.18) * entries
    return jnp.clip(entries, min=-reach, max=reach).astype(kind)


def setup_inputs(seed: int = 0) -> dict:
    splits = jax.random.split(jax.random.key(seed), 5)
    return {
        "green": normal_values(splits[0], (TIMES, ORB, ORB), 0.45, 4.0, ((0, 2),)),
        "factors": normal_values(splits[1], (AUX, ORB), ORB ** -0.5, 0.1875, ((0, 16),)),
        "pattern": plant((jax.random.randint(splits[2], (AUX // BLOCK, ORB // BLOCK), 0, 4) < 3).astype(jnp.int32), jax.random.fold_in(splits[2], 1), 0, 1),
        "coulomb": jnp.clip(jnp.exp(math.log(2.0) - 1.3862944 * jax.random.uniform(splits[3], (AUX,), jnp.float32) ** block_levels(splits[3], (AUX,), ((0, 16),), -0.2, 0.2)), 0.5, 2.0),
    }


def reference(green, factors, pattern, coulomb):
    mask = jnp.repeat(jnp.repeat(pattern, BLOCK, axis=0), BLOCK, axis=1)
    masked = factors * mask.astype(factors.dtype)

    def project(gmat):
        left = jnp.dot(masked, gmat, preferred_element_type=jnp.float32).astype(jnp.bfloat16)
        right = jnp.dot(masked, gmat.T, preferred_element_type=jnp.float32).astype(jnp.bfloat16)
        return left, right

    lefts, rights = lax.map(project, green)
    mirrored = jnp.roll(rights, TIMES // 2, axis=0)

    def self_energy(pair):
        left, right = pair
        aux_green = jnp.dot(left, masked.T, preferred_element_type=jnp.float32)
        mirror = jnp.dot(right, masked.T, preferred_element_type=jnp.float32)
        chi = -aux_green * mirror
        kernel = (aux_green * coulomb[:, None] * chi * coulomb[None, :]).astype(jnp.bfloat16)
        carried = jnp.dot(kernel, masked, preferred_element_type=jnp.float32).astype(jnp.bfloat16)
        return -jnp.dot(masked.T, carried, preferred_element_type=jnp.float32)

    sigma = lax.map(self_energy, (lefts, mirrored))
    return jnp.transpose(sigma, (1, 0, 2))
```

```python
import functools

import jax
import jax.numpy as jnp
from jax import lax
from jax.experimental import pallas as pl
from jax.experimental.pallas import tpu as pltpu
from jax.sharding import PartitionSpec as P

MESH = pl.DeviceIdType.MESH
F32, BF16 = jnp.float32, jnp.bfloat16


def turned(p):
    return p + lax.div(p, 2) * (1 - 2 * lax.rem(p, 2))


def dot(a, b, da, db):
    return lax.dot_general(a, b, (((da,), (db,)), ((), ())), preferred_element_type=F32)


def kernel(cfg, pattern, factors, coul, halves, green_hbm, out,
           pm, rows, weights, pweights, green, psend, lhs, cp, kern, car, sig,
           csend, crecv, xsend, xrecv, zsend, zrecv,
           gsem, z_s, z_r, y_s, y_r, b_s, b_r, s_s, s_r, w_s, w_r, pw_s, pw_r,
           m_s, m_r, p_s, p_r, f_s, f_r, rc_s, rc_r, rx_s, rx_r, rz_s, rz_r):
    Z, X, HP = cfg
    T, O = green.shape[0], green.shape[1]
    U = T // 2
    R2 = pm.shape[2]
    R = 2 * R2
    PR = R2 // HP
    OUT = out.shape[1]
    CH = 2 * X * OUT
    tms = lax.axis_size("tm")
    a, tmi = lax.axis_index("aux"), lax.axis_index("tm")
    c = lax.rem(a, 2)
    x = lax.rem(lax.div(a, 2), X)
    z = lax.div(a, 2 * X)
    pos = turned(z)
    upper = lax.div(tmi, tms // 2)
    partner = lax.rem(tmi + tms // 2, tms)
    plane = lax.rem(tmi, 2)
    mate = tmi + 1 - 2 * plane

    def dev(z_, x_, c_):
        return (z_ * X + x_) * 2 + c_

    def xo(e):
        return lax.rem(x + e, X)

    def zo(f):
        return lax.rem(z + f, Z)

    def ring(k):
        return turned(lax.rem(pos + k, Z))

    sibling = dev(z, x, 1 - c)
    nextd = dev(ring(1), x, c)
    sent = []

    def send(src, dst, s, r, **where):
        copy = pltpu.make_async_remote_copy(
            src_ref=src, dst_ref=dst, send_sem=s, recv_sem=r,
            device_id=where, device_id_type=MESH)
        copy.start()
        sent.append(copy)
        return copy

    def slot(j):
        return (1 - upper) * U + j if j < U else upper * U + j - U

    loads = [pltpu.make_async_copy(green_hbm.at[slot(j)], green.at[j], gsem.at[j]) for j in range(T)]
    for copy in loads:
        copy.start()

    barrier = pltpu.get_barrier_semaphore()
    friends = [{"aux": dev(zo(f), x, c)} for f in range(1, Z)]
    friends += [{"aux": dev(zo(f), x, 1 - c)} for f in range(Z)]
    friends += [{"aux": dev(z, xo(e), c)} for e in range(1, X)]
    friends += [{"aux": dev(zo(f), x, c), "tm": partner} for f in range(Z)]
    if tms > 2:
        friends += [{"tm": mate}]
    for where in friends:
        pl.semaphore_signal(barrier, inc=1, device_id=where, device_id_type=MESH)

    brows = R // pattern.shape[0]
    bcols = O // pattern.shape[1]
    step = min(brows, R2)
    for r0 in range(0, R, step):
        for j in range(pattern.shape[1]):
            rs, cs = pl.ds(r0, step), pl.ds(j * bcols, bcols)
            part = (factors[rs, cs].astype(F32) * pattern[r0 // brows, j].astype(F32)).astype(BF16)
            to = pl.ds(r0 % R2, step)
            pm[0, r0 // R2, to, cs] = part
            rows[0, r0 // R2, 0, to, cs] = part
    weights[0, 0] = halves[...]
    pweights[0] = coul[...]
    pl.semaphore_wait(barrier, len(friends))

    def cut(i):
        return pl.ds(i * PR, PR)

    zc, yc, sc, wc, pwc, mc, pc, fc = {}, {}, {}, {}, {}, {}, {}, {}

    for i in range(HP):
        zc[1, 0, i] = send(pm.at[0, plane, cut(i)], rows.at[1, plane, 0, cut(i)],
                           z_s.at[1, 0, i], z_r.at[1, 0, i], aux=nextd)
    for e in range(1, X):
        for h in range(2):
            mc[e, h] = send(pm.at[0, h], pm.at[X - e, h], m_s.at[e, h], m_r.at[e, h],
                            aux=dev(z, xo(e), c))
    for h in range(2):
        sc[0, h, 0] = send(pm.at[0, h], rows.at[0, h, 1], s_s.at[0, h, 0], s_r.at[0, h, 0], aux=sibling)
    for e in range(1, X):
        pwc[e] = send(coul, pweights.at[X - e], pw_s.at[e], pw_r.at[e], aux=dev(z, xo(e), c))
    for k in range(Z):
        for s in range(2):
            if k + s:
                wc[k, s] = send(halves, weights.at[k, s], w_s.at[k, s], w_r.at[k, s],
                                aux=dev(ring(k), x, c + s * (1 - 2 * c)))

    def project(g, e, store):
        def run(first):
            def one(j, carry):
                at = pl.ds(pl.multiple_of(j * 256, 256), 256)
                m = pm[e].reshape(R, O)
                if first:
                    value = dot(m, green[g, :, at], 1, 0)
                else:
                    value = dot(m, green[g, at, :], 1, 1)
                store(at, value.astype(BF16))
                return carry
            lax.fori_loop(0, O // 256, one, 0)

        pl.when(upper == 0)(lambda: run(True))
        pl.when(upper == 1)(lambda: run(False))

    def to_partner(u):
        loads[u].wait()

        def store(at, value):
            psend[u, 0, :, at] = value[:R2]
            psend[u, 1, :, at] = value[R2:]
        project(u, 0, store)
        for h in range(2):
            for i in range(HP):
                pc[u, h, i] = send(psend.at[u, h, cut(i)], lhs.at[u, h, upper, cut(i)],
                                   p_s.at[u, h, i], p_r.at[u, h, i], tm=partner)

    def keep(u, e):
        def store(at, value):
            lhs[u, 2 * e, upper, :, at] = value[:R2]
            lhs[u, 2 * e + 1, upper, :, at] = value[R2:]
        project(U + u, e, store)

    for u in range(U):
        to_partner(u)
    for u in range(U):
        loads[U + u].wait()
        keep(u, 0)

    def half_of(w):
        return plane if w == 0 else 1 - plane

    def across(k, w, i):
        half = half_of(w)
        sc[k, w, i] = send(rows.at[k, half, 0, cut(i)], rows.at[k, half, 1, cut(i)],
                           s_s.at[k, w, i], s_r.at[k, w, i], aux=sibling)

    def forward(k, w, i):
        half = half_of(w)
        zc[k + 1, w, i] = send(rows.at[k, half, 0, cut(i)], rows.at[k + 1, half, 0, cut(i)],
                               z_s.at[k + 1, w, i], z_r.at[k + 1, w, i], aux=nextd)

    def share(k, i):
        yc[k, i] = send(rows.at[k, plane, 0, cut(i)], rows.at[k, plane, 0, cut(i)],
                        y_s.at[k, i], y_r.at[k, i], tm=mate)

    def on_z(k, w, i, share_now=True):
        zc[k, w, i].wait_recv()
        if k < Z - 1:
            forward(k, w, i)
            if share_now:
                share(k, i)
        across(k, w, i)

    def on_y(k, i):
        yc[k, i].wait_recv()
        if k == Z - 2:
            forward(k, 1, i)
        across(k, 1, i)

    def on_p(u, h, i):
        pc[u, h, i].wait_recv()
        for e in range(1, X):
            at = lhs.at[u, h, 1 - upper, cut(i)]
            fc[u, e, h, i] = send(at, lhs.at[u, 2 * (X - e) + h, 1 - upper, cut(i)],
                                  f_s.at[u, e, h, i], f_r.at[u, e, h, i], aux=dev(z, xo(e), c))

    waited = set()

    def once(*copies):
        for copy in copies:
            if id(copy) not in waited:
                waited.add(id(copy))
                copy.wait_recv()

    def set_cp(e):
        cp[2 * e] = jnp.transpose(jnp.broadcast_to(pweights[e], (R, R)))[:R2]
        cp[2 * e + 1] = jnp.transpose(jnp.broadcast_to(pweights[e], (R, R)))[R2:]

    def others(e):
        for h in range(2):
            once(mc[e, h])
        once(pwc[e])
        set_cp(e)
        for u in range(U):
            keep(u, e)

    def need(k, w):
        if k == 0:
            once(sc[0, w, 0])
        else:
            for i in range(HP):
                once(sc[k, w, i])
        for s in range(2):
            if k + s:
                once(wc[k, s])

    def tiles(p0, pn, k, w):
        need(k, w)
        half = w if k == 0 else half_of(w)
        at = pl.ds(pl.multiple_of((k * 2 + half) * R, R), R)
        g = min(pn, 2)

        def one(n, carry):
            u, p = lax.div(n, pn // g), p0 + g * lax.rem(n, pn // g)
            both = dot(lhs[u, pl.ds(p, g)].reshape(g * R, O), rows[k, half].reshape(R, O), 1, 1)
            wq = jnp.concatenate([weights[k, 0, half], weights[k, 1, half]], axis=1)
            for i in range(g):
                ax, bx = both[i * R:i * R + R2], both[i * R + R2:(i + 1) * R]
                w_ = ax * bx * (cp[p + i] * wq)
                to = pl.ds(pl.multiple_of((p + i) * R2, R2), R2)
                kern[u, 0, to, at] = (w_ * ax).astype(BF16)
                kern[u, 1, to, at] = (w_ * bx).astype(BF16)
            return carry
        lax.fori_loop(0, U * (pn // g), one, 0)

    todo = []

    def plan(when, what, *args):
        todo.append((when, len(todo), what, args))

    def run_plan():
        for _, _, what, args in sorted(todo, key=lambda item: item[:2]):
            what(*args)
        todo.clear()

    PT, L = 5.6 / HP, 1.6
    for i in range(HP):
        plan(PT * (i + 1) + L, on_z, 1, 0, i, False)
        plan(5.6 + PT * (i + 1) + L, on_z, 2, 0, i)
        plan(11.2 + PT * (i + 1) + L, on_z, 3, 0, i)
        plan(16.8 + PT * (i + 1) + L, on_z, 3, 1, i)
        plan(12.8 + PT * (i + 1) + L + 0.1, on_y, 2, i)
        plan(18.4 + PT * (i + 1) + L, on_y, 1, i)
        plan(5.6 + PT * HP + L + 0.05, share, 1, i)
        for h in range(2):
            plan(0.8 + (5.6 * h + PT * (i + 1)) + L + 0.05, lambda h, i: [on_p(u, h, i) for u in range(U)], h, i)
    for e in range(1, X):
        plan(13.0, others, e)
    plan(1.0, set_cp, 0)
    t0 = 13.9
    plan(t0, tiles, 0, 2, 0, 0)
    plan(t0, tiles, 0, 2, 0, 1)
    plan(t0 + 0.3, tiles, 0, 2, 1, 0)
    plan(t0 + 1.5, tiles, 0, 2, 2, 0)
    plan(19.8, tiles, 0, 2, 3, 0)
    plan(20.7, tiles, 0, 2, 2, 1)

    def got(h):
        for u in range(U):
            for e in range(1, X):
                for i in range(HP):
                    once(fc[u, e, h, i])

    def rest(h, units):
        got(h)
        for e in range(1, X):
            for k, w in units:
                tiles(2 * e + h, 1, k, w)
    plan(18.9, rest, 0, [(0, 0), (0, 1), (1, 0), (2, 0)])
    plan(22.7, rest, 0, [(3, 0), (2, 1)])
    early = [(0, 0), (0, 1), (1, 0), (2, 0), (3, 0), (2, 1)]
    plan(24.7, rest, 1, early)
    plan(26.0, tiles, 0, 2 * X, 3, 1)
    plan(26.6, tiles, 0, 2 * X, 1, 1)
    run_plan()

    def carried(u, typ, at):
        return dot(kern[u, typ], rows[:, :, :, :, at].reshape(Z * 2 * R, 256), 1, 0).astype(BF16)

    def all_carried(u):
        def one(j, carry):
            at = pl.ds(pl.multiple_of(j * 256, 256), 256)
            car[u, :, at] = carried(u, 0, at)
            return carry
        lax.fori_loop(0, O // 256, one, 0)

    cross, xc, zs = {}, {}, {}

    def stage_a(q, u, typ, f):
        at = pl.ds(pl.multiple_of(zo(f) * CH, CH), CH)
        if typ:
            def part(n, carry):
                cols = pl.ds(pl.multiple_of(n * 256, 256), 256)
                src = pl.ds(pl.multiple_of(zo(f) * CH + n * 256, 256), 256)
                car[U, :, cols] = carried(u, 1, src)
                return carry
            lax.fori_loop(0, CH // 256, part, 0)

        def one(j, carry):
            to = pl.ds(pl.multiple_of(j * 512, 512), 512)
            if typ:
                value = dot(car[U, :, pl.ds(0, CH)], pm[:, :, :, to].reshape(X * R, 512), 0, 0)
            else:
                value = dot(pm[:, :, :, at].reshape(X * R, CH), car[u, :, to], 0, 0)
            sig[q, :, to] = value
            return carry
        lax.fori_loop(0, O // 512, one, 0)
        for g in range(X):
            mine = pl.ds(pl.multiple_of((g * 2 + 1 - c) * OUT, OUT), OUT)
            csend[q, g] = sig[q, mine, :].astype(BF16)
        cross[q] = send(csend.at[q], crecv.at[q], rc_s.at[q], rc_r.at[q], aux=sibling)

    def summed(q, g):
        at = pl.ds(pl.multiple_of((g * 2 + c) * OUT, OUT), OUT)
        return sig[q, at, :] + crecv[q, g].astype(F32)

    def stage_b(q):
        cross[q].wait_recv()
        for e in range(1, X):
            xsend[q, e - 1] = summed(q, xo(e)).astype(BF16)
            xc[q, e] = send(xsend.at[q, e - 1], xrecv.at[q, e - 1], rx_s.at[q, e - 1],
                            rx_r.at[q, e - 1], aux=dev(z, xo(e), c))

    def last(u, typ, f, tm):
        return pltpu.make_async_remote_copy(
            src_ref=zsend.at[u, typ, f], dst_ref=zrecv.at[upper, u, f],
            send_sem=rz_s.at[u, typ, f], recv_sem=rz_r.at[upper, u, f],
            device_id={"aux": dev(zo(f), x, c), "tm": tm}, device_id_type=MESH)

    def stage_c(q, u, typ, f):
        for e in range(1, X):
            xc[q, e].wait_recv()
        value = summed(q, x)
        for e in range(1, X):
            value = value + xrecv[q, e - 1].astype(F32)
        away = (upper - typ) * (upper - typ)
        if f:
            zsend[u, typ, f] = value.astype(BF16)
            copy = last(u, typ, f, tmi + (partner - tmi) * away)
            copy.start()
            sent.append(copy)
        else:
            @pl.when(away == 0)
            def _():
                zrecv[upper, u, 0] = value.astype(BF16)

            @pl.when(away == 1)
            def _():
                zsend[u, typ, 0] = value.astype(BF16)
                last(u, typ, 0, partner).start()

    def stage_d(sh, u):
        value = None
        for f in [2, 1, 3, 0][-Z:]:
            copy = pltpu.make_async_remote_copy(
                src_ref=zsend.at[u, 0, f], dst_ref=zrecv.at[sh, u, f],
                send_sem=rz_s.at[u, 0, f], recv_sem=rz_r.at[sh, u, f],
                device_id={"tm": partner}, device_id_type=MESH)
            if f:
                copy.wait_recv()
            else:
                pl.when(upper != sh)(copy.wait_recv)
            piece = zrecv[sh, u, f].astype(F32)
            value = piece if value is None else value + piece
        out[sh * U + u] = value

    order = [(u, typ, f) for u in range(U) for f in [2, 1, 3, 0] for typ in (1, 0)]
    compute, hop = 0.9, 22.5 / len(order)
    at = 0.0
    for q, (u, typ, f) in enumerate(order):
        if f == 2 and typ == 0:
            plan(at, all_carried, u)
            at += 2.2
        at += compute
        plan(at, stage_a, q, u, typ, f)
        b = at + 1.7
        plan(b, stage_b, q)
        arrived = max(b, compute + 1.7 + hop * q) + hop + 1.8
        plan(arrived, stage_c, q, u, typ, f)
    for u in range(U):
        plan(100.0, stage_d, 0, u)
        plan(100.0, stage_d, 1, u)
    run_plan()
    for copy in sent:
        copy.wait_send()
    for u in range(U):
        for typ in range(2):
            pl.when(upper != typ)(last(u, typ, 0, partner).wait_send)


def local(green, factors, pattern, coulomb):
    n = lax.axis_size("aux")
    T, O, _ = green.shape
    R = factors.shape[0]
    chips = n // 2
    Z = 4
    X = chips // Z
    HP = 2
    R2 = R // 2
    U = T // 2
    OUT = O // n
    CH = 2 * X * OUT
    Q = U * 2 * Z
    dma = pltpu.SemaphoreType.DMA
    vm = pltpu.VMEM
    scratch = [
        vm((X, 2, R2, O), BF16), vm((Z, 2, 2, R2, O), BF16), vm((Z, 2, 2, 1, R2), F32),
        vm((X, 1, R), F32), vm((T, O, O), BF16), vm((U, 2, R2, O), BF16),
        vm((U, 2 * X, 2, R2, O), BF16), vm((2 * X, R2, R), F32),
        vm((U, 2, X * R, Z * 2 * R), BF16), vm((U + 1, X * R, O), BF16), vm((Q, CH, O), F32),
        vm((Q, X, OUT, O), BF16), vm((Q, X, OUT, O), BF16),
        vm((Q, X - 1, OUT, O), BF16), vm((Q, X - 1, OUT, O), BF16),
        vm((U, 2, Z, OUT, O), BF16), vm((2, U, Z, OUT, O), BF16),
        dma((T,)),
        dma((Z, 2, HP)), dma((Z, 2, HP)), dma((Z, HP)), dma((Z, HP)),
        dma((1,)), dma((1,)),
        dma((Z, 2, HP)), dma((Z, 2, HP)), dma((Z, 2)), dma((Z, 2)), dma((X,)), dma((X,)),
        dma((X, 2)), dma((X, 2)), dma((U, 2, HP)), dma((U, 2, HP)),
        dma((U, X, 2, HP)), dma((U, X, 2, HP)),
        dma((Q,)), dma((Q,)), dma((Q, X - 1)), dma((Q, X - 1)),
        dma((U, 2, Z)), dma((2, U, Z)),
    ]
    vmem = pl.BlockSpec(memory_space=pltpu.VMEM)
    result = pl.pallas_call(
        functools.partial(kernel, (Z, X, HP)),
        out_shape=jax.ShapeDtypeStruct((T, OUT, O), F32),
        in_specs=[pl.BlockSpec(memory_space=pltpu.SMEM), vmem, vmem, vmem,
                  pl.BlockSpec(memory_space=pl.ANY)],
        out_specs=vmem,
        scratch_shapes=scratch,
        compiler_params=pltpu.CompilerParams(
            collective_id=0, has_side_effects=True, vmem_limit_bytes=60 * 2**20),
    )(pattern, factors, coulomb.reshape(1, R), coulomb.reshape(2, 1, R2), green)
    return jnp.transpose(result, (1, 0, 2))


def solution(mesh):
    in_specs = (P("tm", None, None), P("aux", None), P("aux", None), P("aux"))
    out_specs = P("aux", "tm", None)
    return jax.shard_map(local, mesh=mesh, in_specs=in_specs, out_specs=out_specs, check_vma=False)
```

```python
import functools

import jax
import jax.numpy as jnp
from jax import lax
from jax.experimental import pallas as pl
from jax.experimental.pallas import tpu as pltpu
from jax.sharding import PartitionSpec as P

MESH = pl.DeviceIdType.MESH
F32, BF16 = jnp.float32, jnp.bfloat16


def turned(p):
    return p + lax.div(p, 2) * (1 - 2 * lax.rem(p, 2))


def dot(a, b, da, db):
    return lax.dot_general(a, b, (((da,), (db,)), ((), ())), preferred_element_type=F32)


def kernel(cfg, pattern, factors, coul, halves, green_hbm, out,
           pm, rows, weights, pweights, green, psend, lhs, cp, kern, car, acc, sig,
           csend, crecv, xsend, xrecv, zsend, zrecv, nrecv, gsend, grecv, tsend, trecv, fin,
           gsem, z_s, z_r, y_s, y_r, s_s, s_r, w_s, w_r, pw_s, pw_r,
           m_s, m_r, p_s, p_r, f_s, f_r, rc_s, rc_r, rx_s, rx_r, rz_s, rz_r,
           rn_s, rn_r, rg_s, rg_r, rt_s, rt_r):
    Z, X, HP = cfg
    T, O = green.shape[0], green.shape[1]
    U = T // 2
    R2 = pm.shape[2]
    R = 2 * R2
    PR = R2 // HP
    OUT = out.shape[1]
    CH = 2 * X * OUT
    tms = lax.axis_size("tm")
    a, tmi = lax.axis_index("aux"), lax.axis_index("tm")
    c = lax.rem(a, 2)
    x = lax.rem(lax.div(a, 2), X)
    z = lax.div(a, 2 * X)
    pos = turned(z)
    upper = lax.div(tmi, tms // 2)
    partner = lax.rem(tmi + tms // 2, tms)
    plane = lax.rem(tmi, 2)
    mate = tmi + 1 - 2 * plane

    def dev(z_, x_, c_):
        return (z_ * X + x_) * 2 + c_

    def xo(e):
        return lax.rem(x + e, X)

    def zo(f):
        return lax.rem(z + f, Z)

    def ring(k):
        return turned(lax.rem(pos + k, Z))

    sibling = dev(z, x, 1 - c)
    nextd = dev(ring(1), x, c)
    sent = []

    def send(src, dst, s, r, **where):
        copy = pltpu.make_async_remote_copy(
            src_ref=src, dst_ref=dst, send_sem=s, recv_sem=r,
            device_id=where, device_id_type=MESH)
        copy.start()
        sent.append(copy)
        return copy

    def slot(j):
        return (1 - upper) * U + j if j < U else upper * U + j - U

    loads = [pltpu.make_async_copy(green_hbm.at[slot(j)], green.at[j], gsem.at[j]) for j in range(T)]
    for copy in loads:
        copy.start()

    barrier = pltpu.get_barrier_semaphore()
    friends = [{"aux": dev(zo(f), x, c)} for f in range(1, Z)]
    friends += [{"aux": dev(zo(f), x, 1 - c)} for f in range(Z)]
    friends += [{"aux": dev(z, xo(e), c)} for e in range(1, X)]
    friends += [{"tm": partner}]
    if tms > 2:
        friends += [{"tm": mate}]
    for where in friends:
        pl.semaphore_signal(barrier, inc=1, device_id=where, device_id_type=MESH)

    brows = R // pattern.shape[0]
    bcols = O // pattern.shape[1]
    step = min(brows, R2)
    for r0 in range(0, R, step):
        for j in range(pattern.shape[1]):
            rs, cs = pl.ds(r0, step), pl.ds(j * bcols, bcols)
            part = (factors[rs, cs].astype(F32) * pattern[r0 // brows, j].astype(F32)).astype(BF16)
            to = pl.ds(r0 % R2, step)
            pm[0, r0 // R2, to, cs] = part
            rows[0, r0 // R2, 0, to, cs] = part
    weights[0, 0] = halves[...]
    pweights[0] = coul[...]
    pl.semaphore_wait(barrier, len(friends))

    def cut(i):
        return pl.ds(i * PR, PR)

    zc, yc, sc, wc, pwc, mc, pc, fc = {}, {}, {}, {}, {}, {}, {}, {}

    for i in range(HP):
        zc[1, 0, i] = send(pm.at[0, plane, cut(i)], rows.at[1, plane, 0, cut(i)],
                           z_s.at[1, 0, i], z_r.at[1, 0, i], aux=nextd)
    for e in range(1, X):
        for h in range(2):
            mc[e, h] = send(pm.at[0, h], pm.at[X - e, h], m_s.at[e, h], m_r.at[e, h],
                            aux=dev(z, xo(e), c))
    for h in range(2):
        sc[0, h, 0] = send(pm.at[0, h], rows.at[0, h, 1], s_s.at[0, h, 0], s_r.at[0, h, 0], aux=sibling)
    for e in range(1, X):
        pwc[e] = send(coul, pweights.at[X - e], pw_s.at[e], pw_r.at[e], aux=dev(z, xo(e), c))
    for k in range(Z):
        for s in range(2):
            if k + s:
                wc[k, s] = send(halves, weights.at[k, s], w_s.at[k, s], w_r.at[k, s],
                                aux=dev(ring(k), x, c + s * (1 - 2 * c)))

    def project(g, e, turn, store):
        def one(j, carry):
            at = pl.ds(pl.multiple_of(j * 256, 256), 256)
            m = pm[e].reshape(R, O)
            value = dot(m, green[g, at, :], 1, 1) if turn else dot(m, green[g, :, at], 1, 0)
            store(at, value.astype(BF16))
            return carry
        lax.fori_loop(0, O // 256, one, 0)

    def to_partner(u):
        loads[u].wait()

        def store(at, value):
            psend[u, 0, :, at] = value[:R2]
            psend[u, 1, :, at] = value[R2:]
        project(u, 0, True, store)
        for h in range(2):
            for i in range(HP):
                pc[u, h, i] = send(psend.at[u, h, cut(i)], lhs.at[u, h, 1, cut(i)],
                                   p_s.at[u, h, i], p_r.at[u, h, i], tm=partner)

    def keep(u, e):
        def store(at, value):
            lhs[u, 2 * e, 0, :, at] = value[:R2]
            lhs[u, 2 * e + 1, 0, :, at] = value[R2:]
        project(U + u, e, False, store)

    for u in range(U):
        to_partner(u)
    for u in range(U):
        loads[U + u].wait()
        keep(u, 0)

    def half_of(w):
        return plane if w == 0 else 1 - plane

    def across(k, w, i):
        half = half_of(w)
        sc[k, w, i] = send(rows.at[k, half, 0, cut(i)], rows.at[k, half, 1, cut(i)],
                           s_s.at[k, w, i], s_r.at[k, w, i], aux=sibling)

    def forward(k, w, i):
        half = half_of(w)
        zc[k + 1, w, i] = send(rows.at[k, half, 0, cut(i)], rows.at[k + 1, half, 0, cut(i)],
                               z_s.at[k + 1, w, i], z_r.at[k + 1, w, i], aux=nextd)

    def share(k, i):
        yc[k, i] = send(rows.at[k, plane, 0, cut(i)], rows.at[k, plane, 0, cut(i)],
                        y_s.at[k, i], y_r.at[k, i], tm=mate)

    def on_z(k, w, i, share_now=True):
        zc[k, w, i].wait_recv()
        if k < Z - 1:
            forward(k, w, i)
            if share_now:
                share(k, i)
        across(k, w, i)

    def on_y(k, i):
        yc[k, i].wait_recv()
        if k == Z - 2:
            forward(k, 1, i)
        across(k, 1, i)

    def on_p(u, h, i):
        pc[u, h, i].wait_recv()
        for e in range(1, X):
            fc[u, e, h, i] = send(lhs.at[u, h, 1, cut(i)], lhs.at[u, 2 * (X - e) + h, 1, cut(i)],
                                  f_s.at[u, e, h, i], f_r.at[u, e, h, i], aux=dev(z, xo(e), c))

    waited = set()

    def once(*copies):
        for copy in copies:
            if id(copy) not in waited:
                waited.add(id(copy))
                copy.wait_recv()

    def set_cp(e):
        cp[2 * e] = jnp.transpose(jnp.broadcast_to(pweights[e], (R, R)))[:R2]
        cp[2 * e + 1] = jnp.transpose(jnp.broadcast_to(pweights[e], (R, R)))[R2:]

    def others(e):
        for h in range(2):
            once(mc[e, h])
        once(pwc[e])
        set_cp(e)
        for u in range(U):
            keep(u, e)

    def need(k, w):
        if k == 0:
            once(sc[0, w, 0])
        else:
            for i in range(HP):
                once(sc[k, w, i])
        for s in range(2):
            if k + s:
                once(wc[k, s])

    def tiles(p0, pn, k, w):
        need(k, w)
        half = w if k == 0 else half_of(w)
        at = pl.ds(pl.multiple_of((k * 2 + half) * R, R), R)
        g = min(pn, 2)

        def one(n, carry):
            u, p = lax.div(n, pn // g), p0 + g * lax.rem(n, pn // g)
            both = dot(lhs[u, pl.ds(p, g)].reshape(g * R, O), rows[k, half].reshape(R, O), 1, 1)
            wq = jnp.concatenate([weights[k, 0, half], weights[k, 1, half]], axis=1)
            for i in range(g):
                ax, bx = both[i * R:i * R + R2], both[i * R + R2:(i + 1) * R]
                w_ = ax * bx * (cp[p + i] * wq)
                to = pl.ds(pl.multiple_of((p + i) * R2, R2), R2)
                kern[u, 0, to, at] = (w_ * ax).astype(BF16)
                kern[u, 1, to, at] = (w_ * bx).astype(BF16)
            return carry
        lax.fori_loop(0, U * (pn // g), one, 0)

    def early_carried(u, typ):
        def one(j, carry):
            at = pl.ds(pl.multiple_of(j * 256, 256), 256)
            value = None
            for k in range(Z):
                if k in (0, 2):
                    mine, part = pl.ds(2 * k * R, 2 * R), rows[k, :, :, :, at].reshape(2 * R, 256)
                else:
                    mine = pl.ds(pl.multiple_of((k * 2 + plane) * R, R), R)
                    part = rows[k, plane, :, :, at].reshape(R, 256)
                term = dot(kern[u, typ, pl.ds(0, R), mine], part, 1, 0)
                value = term if value is None else value + term
            acc[u, typ, :, at] = value
            return carry
        lax.fori_loop(0, O // 256, one, 0)

    todo = []

    def plan(when, what, *args):
        todo.append((when, len(todo), what, args))

    def run_plan():
        for _, _, what, args in sorted(todo, key=lambda item: item[:2]):
            what(*args)
        todo.clear()

    PT, L = 5.6 / HP, 1.6
    for i in range(HP):
        plan(PT * (i + 1) + L, on_z, 1, 0, i, False)
        plan(5.6 + PT * (i + 1) + L, on_z, 2, 0, i)
        plan(11.2 + PT * (i + 1) + L, on_z, 3, 0, i)
        plan(16.8 + PT * (i + 1) + L, on_z, 3, 1, i)
        plan(12.8 + PT * (i + 1) + L + 0.1, on_y, 2, i)
        plan(18.4 + PT * (i + 1) + L, on_y, 1, i)
        plan(5.6 + PT * HP + L + 0.05, share, 1, i)
        for h in range(2):
            plan(0.8 + (5.6 * h + PT * (i + 1)) + L + 0.05, lambda h, i: [on_p(u, h, i) for u in range(U)], h, i)
    for e in range(1, X):
        plan(13.0, others, e)
    plan(1.0, set_cp, 0)
    t0 = 13.9
    plan(t0, tiles, 0, 2, 0, 0)
    plan(t0, tiles, 0, 2, 0, 1)
    plan(t0 + 0.3, tiles, 0, 2, 1, 0)
    plan(t0 + 1.5, tiles, 0, 2, 2, 0)
    plan(19.8, tiles, 0, 2, 3, 0)
    plan(20.7, tiles, 0, 2, 2, 1)

    for u in range(U):
        plan(21.4, early_carried, u, 1)
        plan(21.4 + 0.9, early_carried, u, 0)

    def got(h):
        for u in range(U):
            for e in range(1, X):
                for i in range(HP):
                    once(fc[u, e, h, i])

    def rest(h, units):
        got(h)
        for e in range(1, X):
            for k, w in units:
                tiles(2 * e + h, 1, k, w)
    plan(18.9, rest, 0, [(0, 0), (0, 1), (1, 0), (2, 0)])
    plan(22.7, rest, 0, [(3, 0), (2, 1)])
    early = [(0, 0), (0, 1), (1, 0), (2, 0), (3, 0), (2, 1)]
    plan(24.7, rest, 1, early)
    plan(26.0, tiles, 0, 2 * X, 3, 1)
    plan(26.6, tiles, 0, 2 * X, 1, 1)
    run_plan()

    def column(k, half):
        return pl.ds(pl.multiple_of((k * 2 + half) * R, R), R)

    def carried(u, typ, at, width):
        late = 1 - plane
        near = acc[u, typ, :, at]
        for k in (1, Z - 1):
            near = near + dot(kern[u, typ, pl.ds(0, R), column(k, late)], rows[k, late, :, :, at].reshape(R, width), 1, 0)
        far = dot(kern[u, typ, pl.ds(R, (X - 1) * R)], rows[:, :, :, :, at].reshape(Z * 2 * R, width), 1, 0)
        return jnp.concatenate([near.astype(BF16), far.astype(BF16)], axis=0)

    def block(u, n):
        width = O // 4
        at = pl.ds(n * width, width)
        car[u, :, at] = carried(u, 0, at, width)

    DIAG, CROSS, NB, OWN = range(4)
    ZF, DIRECT = (1,), ()
    nbz = z + 1 - 2 * lax.rem(z, 2)
    target = [lax.rem(nbz + 2, Z), zo(2), nbz, z]
    nbd, crossd = dev(nbz, x, c), dev(zo(2), x, c)
    cross, xc, nc, gc, zf, tc = {}, {}, {}, {}, {}, {}

    def index(u, typ, d):
        return (u * 2 + typ) * 4 + d

    def stage_a(u, typ, d):
        q = index(u, typ, d)
        base = target[d] * CH
        at = pl.ds(pl.multiple_of(base, CH), CH)
        if typ:
            car[U, :, pl.ds(0, CH)] = carried(u, 1, at, CH)
            sig[q] = dot(car[U, :, pl.ds(0, CH)], pm[...].reshape(X * R, O), 0, 0)
        else:
            sig[q] = dot(pm[:, :, :, at].reshape(X * R, CH), car[u], 0, 0)
        for g in range(X):
            mine = pl.ds(pl.multiple_of((g * 2 + 1 - c) * OUT, OUT), OUT)
            csend[q, g] = sig[q, mine, :].astype(BF16)
        cross[q] = send(csend.at[q], crecv.at[q], rc_s.at[q], rc_r.at[q], aux=sibling)

    def summed(u, typ, d, g):
        q = index(u, typ, d)
        at = pl.ds(pl.multiple_of((g * 2 + c) * OUT, OUT), OUT)
        value = sig[q, at, :] + crecv[q, g].astype(F32)
        if d == OWN and typ in ZF:
            value = value + grecv[u, typ, g].astype(F32)
        return value

    def stage_g(u, typ, part):
        once(cross[index(u, typ, NB)])
        for g in range(X):
            if g * 2 // X == part:
                gsend[u, typ, g] = summed(u, typ, NB, g).astype(BF16)
                gc[u, typ, g] = send(gsend.at[u, typ, g], grecv.at[u, typ, g], rg_s.at[u, typ, g],
                                     rg_r.at[u, typ, g], aux=nbd)

    def stage_b(u, typ, d):
        q = index(u, typ, d)
        once(cross[q])
        if d == OWN and typ in ZF:
            once(*[gc[u, typ, g] for g in range(X)])
        for e in range(1, X):
            xsend[q, e - 1] = summed(u, typ, d, xo(e)).astype(BF16)
            xc[q, e] = send(xsend.at[q, e - 1], xrecv.at[q, e - 1], rx_s.at[q, e - 1],
                            rx_r.at[q, e - 1], aux=dev(z, xo(e), c))

    def stage_c(u, typ, d):
        q = index(u, typ, d)
        for e in range(1, X):
            once(xc[q, e])
        value = summed(u, typ, d, x)
        for e in range(1, X):
            value = value + xrecv[q, e - 1].astype(F32)
        if d == CROSS and typ not in DIRECT:
            once(nc[u, typ])
            value = value + nrecv[u, typ].astype(F32)
        if d == OWN:
            fin[u, typ] = value
            return
        zsend[q] = value.astype(BF16)
        if d == DIAG and typ in DIRECT:
            zf[u, typ, 2] = send(zsend.at[q], zrecv.at[u, typ, 2], rz_s.at[u, typ, 2],
                                 rz_r.at[u, typ, 2], aux=dev(target[DIAG], x, c))
        elif d == DIAG:
            nc[u, typ] = send(zsend.at[q], nrecv.at[u, typ], rn_s.at[u, typ], rn_r.at[u, typ], aux=nbd)
        else:
            to = 0 if d == NB else 1
            zf[u, typ, to] = send(zsend.at[q], zrecv.at[u, typ, to], rz_s.at[u, typ, to],
                                  rz_r.at[u, typ, to], aux=nbd if d == NB else crossd)

    def stage_d(u, typ):
        value = fin[u, typ]
        for to in (2, 1, 0):
            if (to == 0 and typ not in ZF) or to == 1 or (to == 2 and typ in DIRECT):
                once(zf[u, typ, to])
                value = value + zrecv[u, typ, to].astype(F32)
        if typ:
            tsend[u] = value.astype(BF16)
            tc[u] = send(tsend.at[u], trecv.at[u], rt_s.at[u], rt_r.at[u], tm=partner)
        else:
            out[upper * U + u] = value

    def stage_e(u):
        once(tc[u])
        out[(1 - upper) * U + u] = trecv[u].astype(F32)

    steps = (
        ("A", 1, DIAG), ("A", 1, NB), ("B", 1, DIAG), ("A", 1, CROSS), ("G", 1, 0), ("W", 0),
        ("B", 1, CROSS), ("W", 1), ("W", 2), ("W", 3), ("A", 0, DIAG), ("C", 1, DIAG),
        ("G", 1, 1), ("A", 0, CROSS), ("B", 0, DIAG), ("A", 1, OWN), ("B", 0, CROSS), ("A", 0, NB),
        ("C", 1, CROSS), ("A", 0, OWN), ("B", 1, OWN), ("B", 0, NB), ("C", 0, DIAG), ("C", 0, CROSS),
        ("B", 0, OWN), ("C", 1, OWN), ("D", 1), ("C", 0, NB), ("C", 0, OWN), ("E",),
        ("D", 0),
    )
    run = {"A": stage_a, "B": stage_b, "C": stage_c, "D": stage_d, "E": stage_e, "G": stage_g, "W": block}
    for u in range(U):
        for step in steps:
            run[step[0]](u, *step[1:])
    for copy in sent:
        copy.wait_send()


def local(green, factors, pattern, coulomb):
    n = lax.axis_size("aux")
    T, O, _ = green.shape
    R = factors.shape[0]
    chips = n // 2
    Z = 4
    X = chips // Z
    HP = 2
    R2 = R // 2
    U = T // 2
    OUT = O // n
    CH = 2 * X * OUT
    Q = U * 2 * Z
    dma = pltpu.SemaphoreType.DMA
    vm = pltpu.VMEM
    scratch = [
        vm((X, 2, R2, O), BF16), vm((Z, 2, 2, R2, O), BF16), vm((Z, 2, 2, 1, R2), F32),
        vm((X, 1, R), F32), vm((T, O, O), BF16), vm((U, 2, R2, O), BF16),
        vm((U, 2 * X, 2, R2, O), BF16), vm((2 * X, R2, R), F32),
        vm((U, 2, X * R, Z * 2 * R), BF16), vm((U + 1, X * R, O), BF16), vm((U, 2, R, O), F32), vm((Q, CH, O), F32),
        vm((Q, X, OUT, O), BF16), vm((Q, X, OUT, O), BF16),
        vm((Q, X - 1, OUT, O), BF16), vm((Q, X - 1, OUT, O), BF16),
        vm((Q, OUT, O), BF16), vm((U, 2, 3, OUT, O), BF16), vm((U, 2, OUT, O), BF16),
        vm((U, 2, X, OUT, O), BF16), vm((U, 2, X, OUT, O), BF16),
        vm((U, OUT, O), BF16), vm((U, OUT, O), BF16), vm((U, 2, OUT, O), F32),
        dma((T,)),
        dma((Z, 2, HP)), dma((Z, 2, HP)), dma((Z, HP)), dma((Z, HP)),
        dma((Z, 2, HP)), dma((Z, 2, HP)), dma((Z, 2)), dma((Z, 2)), dma((X,)), dma((X,)),
        dma((X, 2)), dma((X, 2)), dma((U, 2, HP)), dma((U, 2, HP)),
        dma((U, X, 2, HP)), dma((U, X, 2, HP)),
        dma((Q,)), dma((Q,)), dma((Q, X - 1)), dma((Q, X - 1)),
        dma((U, 2, 3)), dma((U, 2, 3)), dma((U, 2)), dma((U, 2)),
        dma((U, 2, X)), dma((U, 2, X)), dma((U,)), dma((U,)),
    ]
    vmem = pl.BlockSpec(memory_space=pltpu.VMEM)
    result = pl.pallas_call(
        functools.partial(kernel, (Z, X, HP)),
        out_shape=jax.ShapeDtypeStruct((T, OUT, O), F32),
        in_specs=[pl.BlockSpec(memory_space=pltpu.SMEM), vmem, vmem, vmem,
                  pl.BlockSpec(memory_space=pl.ANY)],
        out_specs=vmem,
        scratch_shapes=scratch,
        compiler_params=pltpu.CompilerParams(
            collective_id=0, has_side_effects=True, vmem_limit_bytes=60 * 2**20),
    )(pattern, factors, coulomb.reshape(1, R), coulomb.reshape(2, 1, R2), green)
    return jnp.transpose(result, (1, 0, 2))


def solution(mesh):
    in_specs = (P("tm", None, None), P("aux", None), P("aux", None), P("aux"))
    out_specs = P("aux", "tm", None)
    return jax.shard_map(local, mesh=mesh, in_specs=in_specs, out_specs=out_specs, check_vma=False)
```

```python
import functools

import jax
import jax.numpy as jnp
from jax import lax
from jax.experimental import pallas as pl
from jax.experimental.pallas import tpu as pltpu
from jax.sharding import PartitionSpec as P

MESH = pl.DeviceIdType.MESH
F32, BF16 = jnp.float32, jnp.bfloat16


def turned(p):
    return p + lax.div(p, 2) * (1 - 2 * lax.rem(p, 2))


def dot(a, b, da, db):
    return lax.dot_general(a, b, (((da,), (db,)), ((), ())), preferred_element_type=F32)


def kernel(cfg, pattern_hbm, factors_hbm, coul_hbm, halves_hbm, green_hbm, out_hbm,
           pattern, factors, out,           pm, rows, weights, pweights, green, psend, lhs, cp, kern, car, acc, sig,
           csend, crecv, xsend, xrecv, zsend, zrecv, nrecv, gsend, grecv, tsend, trecv, fin,
           gsem, isem, osem, z_s, z_r, y_s, y_r, s_s, s_r, w_s, w_r, pw_s, pw_r,
           m_s, m_r, p_s, p_r, f_s, f_r, rc_s, rc_r, rx_s, rx_r, rz_s, rz_r,
           rn_s, rn_r, rg_s, rg_r, rt_s, rt_r):
    Z, X, HP = cfg
    T, O = green.shape[0], green.shape[1]
    U = T // 2
    R2 = pm.shape[2]
    R = 2 * R2
    PR = R2 // HP
    OUT = out.shape[1]
    CH = 2 * X * OUT
    tms = lax.axis_size("tm")
    a, tmi = lax.axis_index("aux"), lax.axis_index("tm")
    c = lax.rem(a, 2)
    x = lax.rem(lax.div(a, 2), X)
    z = lax.div(a, 2 * X)
    pos = turned(z)
    upper = lax.div(tmi, tms // 2)
    partner = lax.rem(tmi + tms // 2, tms)
    plane = lax.rem(tmi, 2)
    mate = tmi + 1 - 2 * plane

    def dev(z_, x_, c_):
        return (z_ * X + x_) * 2 + c_

    def xo(e):
        return lax.rem(x + e, X)

    def zo(f):
        return lax.rem(z + f, Z)

    def ring(k):
        return turned(lax.rem(pos + k, Z))

    sibling = dev(z, x, 1 - c)
    nextd = dev(ring(1), x, c)
    sent = []

    def send(src, dst, s, r, **where):
        copy = pltpu.make_async_remote_copy(
            src_ref=src, dst_ref=dst, send_sem=s, recv_sem=r,
            device_id=where, device_id_type=MESH)
        copy.start()
        sent.append(copy)
        return copy

    def slot(j):
        return (1 - upper) * U + j if j < U else upper * U + j - U

    loads = [pltpu.make_async_copy(green_hbm.at[slot(j)], green.at[j], gsem.at[j]) for j in range(T)]
    barrier = pltpu.get_barrier_semaphore()
    friends = [{"aux": dev(zo(f), x, c)} for f in range(1, Z)]
    friends += [{"aux": dev(zo(f), x, 1 - c)} for f in range(Z)]
    friends += [{"aux": dev(z, xo(e), c)} for e in range(1, X)]
    friends += [{"tm": partner}]
    if tms > 2:
        friends += [{"tm": mate}]
    for where in friends:
        pl.semaphore_signal(barrier, inc=1, device_id=where, device_id_type=MESH)
    inputs = [(pattern_hbm, pattern), (factors_hbm, factors), (coul_hbm, pweights.at[0]),
              (halves_hbm, weights.at[0, 0])]
    inputs = [pltpu.make_async_copy(src, dst, isem.at[n]) for n, (src, dst) in enumerate(inputs)]
    for copy in inputs + loads:
        copy.start()
    for copy in inputs:
        copy.wait()

    brows = R // pattern.shape[0]
    bcols = O // pattern.shape[1]
    step = min(brows, R2)
    for r0 in range(0, R, step):
        for j in range(pattern.shape[1]):
            rs, cs = pl.ds(r0, step), pl.ds(j * bcols, bcols)
            part = (factors[rs, cs].astype(F32) * pattern[r0 // brows, j].astype(F32)).astype(BF16)
            to = pl.ds(r0 % R2, step)
            pm[0, r0 // R2, to, cs] = part
            rows[0, r0 // R2, 0, to, cs] = part
    pl.semaphore_wait(barrier, len(friends))

    def cut(i):
        return pl.ds(i * PR, PR)

    zc, yc, sc, wc, pwc, mc, pc, fc = {}, {}, {}, {}, {}, {}, {}, {}

    for i in range(HP):
        zc[1, 0, i] = send(pm.at[0, plane, cut(i)], rows.at[1, plane, 0, cut(i)],
                           z_s.at[1, 0, i], z_r.at[1, 0, i], aux=nextd)
    for e in range(1, X):
        for h in range(2):
            mc[e, h] = send(pm.at[0, h], pm.at[X - e, h], m_s.at[e, h], m_r.at[e, h],
                            aux=dev(z, xo(e), c))
    for h in range(2):
        sc[0, h, 0] = send(pm.at[0, h], rows.at[0, h, 1], s_s.at[0, h, 0], s_r.at[0, h, 0], aux=sibling)
    for e in range(1, X):
        pwc[e] = send(pweights.at[0], pweights.at[X - e], pw_s.at[e], pw_r.at[e], aux=dev(z, xo(e), c))
    for k in range(Z):
        for s in range(2):
            if k + s:
                wc[k, s] = send(weights.at[0, 0], weights.at[k, s], w_s.at[k, s], w_r.at[k, s],
                                aux=dev(ring(k), x, c + s * (1 - 2 * c)))

    def project(g, e, turn, store):
        def one(j, carry):
            at = pl.ds(pl.multiple_of(j * 256, 256), 256)
            m = pm[e].reshape(R, O)
            value = dot(m, green[g, at, :], 1, 1) if turn else dot(m, green[g, :, at], 1, 0)
            store(at, value.astype(BF16))
            return carry
        lax.fori_loop(0, O // 256, one, 0)

    def to_partner(u):
        loads[u].wait()

        def store(at, value):
            psend[u, 0, :, at] = value[:R2]
            psend[u, 1, :, at] = value[R2:]
        project(u, 0, True, store)
        for h in range(2):
            for i in range(HP):
                pc[u, h, i] = send(psend.at[u, h, cut(i)], lhs.at[u, h, 1, cut(i)],
                                   p_s.at[u, h, i], p_r.at[u, h, i], tm=partner)

    def keep(u, e):
        def store(at, value):
            lhs[u, 2 * e, 0, :, at] = value[:R2]
            lhs[u, 2 * e + 1, 0, :, at] = value[R2:]
        project(U + u, e, False, store)

    for u in range(U):
        to_partner(u)
    for u in range(U):
        loads[U + u].wait()
        keep(u, 0)

    def half_of(w):
        return plane if w == 0 else 1 - plane

    def across(k, w, i):
        half = half_of(w)
        sc[k, w, i] = send(rows.at[k, half, 0, cut(i)], rows.at[k, half, 1, cut(i)],
                           s_s.at[k, w, i], s_r.at[k, w, i], aux=sibling)

    def forward(k, w, i):
        half = half_of(w)
        zc[k + 1, w, i] = send(rows.at[k, half, 0, cut(i)], rows.at[k + 1, half, 0, cut(i)],
                               z_s.at[k + 1, w, i], z_r.at[k + 1, w, i], aux=nextd)

    def share(k, i):
        yc[k, i] = send(rows.at[k, plane, 0, cut(i)], rows.at[k, plane, 0, cut(i)],
                        y_s.at[k, i], y_r.at[k, i], tm=mate)

    def on_z(k, w, i, share_now=True):
        zc[k, w, i].wait_recv()
        if k < Z - 1:
            forward(k, w, i)
            if share_now:
                share(k, i)
        across(k, w, i)

    def on_y(k, i):
        yc[k, i].wait_recv()
        if k == Z - 2:
            forward(k, 1, i)
        across(k, 1, i)

    def on_p(u, h, i):
        pc[u, h, i].wait_recv()
        for e in range(1, X):
            fc[u, e, h, i] = send(lhs.at[u, h, 1, cut(i)], lhs.at[u, 2 * (X - e) + h, 1, cut(i)],
                                  f_s.at[u, e, h, i], f_r.at[u, e, h, i], aux=dev(z, xo(e), c))

    waited = set()

    def once(*copies):
        for copy in copies:
            if id(copy) not in waited:
                waited.add(id(copy))
                copy.wait_recv()

    def set_cp(e):
        cp[2 * e] = jnp.transpose(jnp.broadcast_to(pweights[e], (R, R)))[:R2]
        cp[2 * e + 1] = jnp.transpose(jnp.broadcast_to(pweights[e], (R, R)))[R2:]

    def others(e):
        for h in range(2):
            once(mc[e, h])
        once(pwc[e])
        set_cp(e)
        for u in range(U):
            keep(u, e)

    def need(k, w):
        if k == 0:
            once(sc[0, w, 0])
        else:
            for i in range(HP):
                once(sc[k, w, i])
        for s in range(2):
            if k + s:
                once(wc[k, s])

    def tiles(p0, pn, k, w):
        need(k, w)
        half = w if k == 0 else half_of(w)
        at = pl.ds(pl.multiple_of((k * 2 + half) * R, R), R)
        g = min(pn, 2)

        def one(n, carry):
            u, p = lax.div(n, pn // g), p0 + g * lax.rem(n, pn // g)
            both = dot(lhs[u, pl.ds(p, g)].reshape(g * R, O), rows[k, half].reshape(R, O), 1, 1)
            wq = jnp.concatenate([weights[k, 0, half], weights[k, 1, half]], axis=1)
            for i in range(g):
                ax, bx = both[i * R:i * R + R2], both[i * R + R2:(i + 1) * R]
                w_ = ax * bx * (cp[p + i] * wq)
                to = pl.ds(pl.multiple_of((p + i) * R2, R2), R2)
                kern[u, 0, to, at] = (w_ * ax).astype(BF16)
                kern[u, 1, to, at] = (w_ * bx).astype(BF16)
            return carry
        lax.fori_loop(0, U * (pn // g), one, 0)

    def early_carried(u, typ):
        def one(j, carry):
            at = pl.ds(pl.multiple_of(j * 256, 256), 256)
            value = None
            for k in range(Z):
                if k in (0, 2):
                    mine, part = pl.ds(2 * k * R, 2 * R), rows[k, :, :, :, at].reshape(2 * R, 256)
                else:
                    mine = pl.ds(pl.multiple_of((k * 2 + plane) * R, R), R)
                    part = rows[k, plane, :, :, at].reshape(R, 256)
                term = dot(kern[u, typ, pl.ds(0, R), mine], part, 1, 0)
                value = term if value is None else value + term
            acc[u, typ, :, at] = value
            return carry
        lax.fori_loop(0, O // 256, one, 0)

    todo = []

    def plan(when, what, *args):
        todo.append((when, len(todo), what, args))

    def run_plan():
        for _, _, what, args in sorted(todo, key=lambda item: item[:2]):
            what(*args)
        todo.clear()

    PT, L = 5.6 / HP, 1.6
    for i in range(HP):
        plan(PT * (i + 1) + L, on_z, 1, 0, i, False)
        plan(5.6 + PT * (i + 1) + L, on_z, 2, 0, i)
        plan(11.2 + PT * (i + 1) + L, on_z, 3, 0, i)
        plan(16.8 + PT * (i + 1) + L, on_z, 3, 1, i)
        plan(12.8 + PT * (i + 1) + L + 0.1, on_y, 2, i)
        plan(18.4 + PT * (i + 1) + L, on_y, 1, i)
        plan(5.6 + PT * HP + L + 0.05, share, 1, i)
        for h in range(2):
            plan(0.8 + (5.6 * h + PT * (i + 1)) + L + 0.05, lambda h, i: [on_p(u, h, i) for u in range(U)], h, i)
    for e in range(1, X):
        plan(13.0, others, e)
    plan(1.0, set_cp, 0)
    t0 = 13.9
    plan(t0, tiles, 0, 2, 0, 0)
    plan(t0, tiles, 0, 2, 0, 1)
    plan(t0 + 0.3, tiles, 0, 2, 1, 0)
    plan(t0 + 1.5, tiles, 0, 2, 2, 0)
    plan(19.8, tiles, 0, 2, 3, 0)
    plan(20.7, tiles, 0, 2, 2, 1)

    for u in range(U):
        plan(21.4, early_carried, u, 1)
        plan(21.4 + 0.9, early_carried, u, 0)

    def got(h):
        for u in range(U):
            for e in range(1, X):
                for i in range(HP):
                    once(fc[u, e, h, i])

    def rest(h, units):
        got(h)
        for e in range(1, X):
            for k, w in units:
                tiles(2 * e + h, 1, k, w)
    plan(18.9, rest, 0, [(0, 0), (0, 1), (1, 0), (2, 0)])
    plan(22.7, rest, 0, [(3, 0), (2, 1)])
    early = [(0, 0), (0, 1), (1, 0), (2, 0), (3, 0), (2, 1)]
    plan(24.7, rest, 1, early)
    plan(26.0, tiles, 0, 2 * X, 3, 1)
    plan(26.6, tiles, 0, 2 * X, 1, 1)
    run_plan()

    def column(k, half):
        return pl.ds(pl.multiple_of((k * 2 + half) * R, R), R)

    def carried(u, typ, at, width):
        late = 1 - plane
        near = acc[u, typ, :, at]
        for k in (1, Z - 1):
            near = near + dot(kern[u, typ, pl.ds(0, R), column(k, late)], rows[k, late, :, :, at].reshape(R, width), 1, 0)
        far = dot(kern[u, typ, pl.ds(R, (X - 1) * R)], rows[:, :, :, :, at].reshape(Z * 2 * R, width), 1, 0)
        return jnp.concatenate([near.astype(BF16), far.astype(BF16)], axis=0)

    def block(u, n):
        width = O // 4
        at = pl.ds(n * width, width)
        car[u, :, at] = carried(u, 0, at, width)

    DIAG, CROSS, NB, OWN = range(4)
    ZF, DIRECT = (1,), ()
    nbz = z + 1 - 2 * lax.rem(z, 2)
    target = [lax.rem(nbz + 2, Z), zo(2), nbz, z]
    nbd, crossd = dev(nbz, x, c), dev(zo(2), x, c)
    cross, xc, nc, gc, zf, tc = {}, {}, {}, {}, {}, {}

    def index(u, typ, d):
        return (u * 2 + typ) * 4 + d

    def stage_a(u, typ, d):
        q = index(u, typ, d)
        base = target[d] * CH
        at = pl.ds(pl.multiple_of(base, CH), CH)
        if typ:
            car[U, :, pl.ds(0, CH)] = carried(u, 1, at, CH)
            sig[q] = dot(car[U, :, pl.ds(0, CH)], pm[...].reshape(X * R, O), 0, 0)
        else:
            sig[q] = dot(pm[:, :, :, at].reshape(X * R, CH), car[u], 0, 0)
        for g in range(X):
            mine = pl.ds(pl.multiple_of((g * 2 + 1 - c) * OUT, OUT), OUT)
            csend[q, g] = sig[q, mine, :].astype(BF16)
        cross[q] = send(csend.at[q], crecv.at[q], rc_s.at[q], rc_r.at[q], aux=sibling)

    def summed(u, typ, d, g):
        q = index(u, typ, d)
        at = pl.ds(pl.multiple_of((g * 2 + c) * OUT, OUT), OUT)
        value = sig[q, at, :] + crecv[q, g].astype(F32)
        if d == OWN and typ in ZF:
            value = value + grecv[u, typ, g].astype(F32)
        return value

    def stage_g(u, typ, part):
        once(cross[index(u, typ, NB)])
        for g in range(X):
            if g * 2 // X == part:
                gsend[u, typ, g] = summed(u, typ, NB, g).astype(BF16)
                gc[u, typ, g] = send(gsend.at[u, typ, g], grecv.at[u, typ, g], rg_s.at[u, typ, g],
                                     rg_r.at[u, typ, g], aux=nbd)

    def stage_b(u, typ, d):
        q = index(u, typ, d)
        once(cross[q])
        if d == OWN and typ in ZF:
            once(*[gc[u, typ, g] for g in range(X)])
        for e in range(1, X):
            xsend[q, e - 1] = summed(u, typ, d, xo(e)).astype(BF16)
            xc[q, e] = send(xsend.at[q, e - 1], xrecv.at[q, e - 1], rx_s.at[q, e - 1],
                            rx_r.at[q, e - 1], aux=dev(z, xo(e), c))

    def stage_c(u, typ, d):
        q = index(u, typ, d)
        for e in range(1, X):
            once(xc[q, e])
        value = summed(u, typ, d, x)
        for e in range(1, X):
            value = value + xrecv[q, e - 1].astype(F32)
        if d == CROSS and typ not in DIRECT:
            once(nc[u, typ])
            value = value + nrecv[u, typ].astype(F32)
        if d == OWN:
            fin[u, typ] = value
            return
        zsend[q] = value.astype(BF16)
        if d == DIAG and typ in DIRECT:
            zf[u, typ, 2] = send(zsend.at[q], zrecv.at[u, typ, 2], rz_s.at[u, typ, 2],
                                 rz_r.at[u, typ, 2], aux=dev(target[DIAG], x, c))
        elif d == DIAG:
            nc[u, typ] = send(zsend.at[q], nrecv.at[u, typ], rn_s.at[u, typ], rn_r.at[u, typ], aux=nbd)
        else:
            to = 0 if d == NB else 1
            zf[u, typ, to] = send(zsend.at[q], zrecv.at[u, typ, to], rz_s.at[u, typ, to],
                                  rz_r.at[u, typ, to], aux=nbd if d == NB else crossd)

    ends = []

    def finish(n, t):
        copy = pltpu.make_async_copy(out.at[t], out_hbm.at[t], osem.at[n])
        copy.start()
        ends.append(copy)

    def stage_d(u, typ):
        value = fin[u, typ]
        for to in (2, 1, 0):
            if (to == 0 and typ not in ZF) or to == 1 or (to == 2 and typ in DIRECT):
                once(zf[u, typ, to])
                value = value + zrecv[u, typ, to].astype(F32)
        if typ:
            tsend[u] = value.astype(BF16)
            tc[u] = send(tsend.at[u], trecv.at[u], rt_s.at[u], rt_r.at[u], tm=partner)
        else:
            out[upper * U + u] = value
            finish(u, upper * U + u)

    def stage_e(u):
        once(tc[u])
        out[(1 - upper) * U + u] = trecv[u].astype(F32)
        finish(U + u, (1 - upper) * U + u)

    steps = (
        ("A", 1, DIAG), ("A", 1, NB), ("B", 1, DIAG), ("A", 1, CROSS), ("G", 1, 0), ("W", 0),
        ("B", 1, CROSS), ("W", 1), ("W", 2), ("W", 3), ("A", 0, DIAG), ("C", 1, DIAG),
        ("G", 1, 1), ("A", 0, CROSS), ("B", 0, DIAG), ("B", 0, CROSS), ("A", 1, OWN), ("A", 0, NB),
        ("C", 1, CROSS), ("B", 0, NB), ("A", 0, OWN), ("B", 1, OWN), ("C", 0, DIAG), ("C", 0, CROSS),
        ("B", 0, OWN), ("C", 0, NB), ("C", 1, OWN), ("D", 1), ("C", 0, OWN), ("E",),
        ("D", 0),
    )
    run = {"A": stage_a, "B": stage_b, "C": stage_c, "D": stage_d, "E": stage_e, "G": stage_g, "W": block}
    for u in range(U):
        for step in steps:
            run[step[0]](u, *step[1:])
    for copy in sent:
        copy.wait_send()
    for copy in ends:
        copy.wait()


def local(green, factors, pattern, coulomb):
    n = lax.axis_size("aux")
    T, O, _ = green.shape
    R = factors.shape[0]
    chips = n // 2
    Z = 4
    X = chips // Z
    HP = 2
    R2 = R // 2
    U = T // 2
    OUT = O // n
    CH = 2 * X * OUT
    Q = U * 2 * Z
    dma = pltpu.SemaphoreType.DMA
    vm = pltpu.VMEM
    scratch = [
        pltpu.SMEM(pattern.shape, jnp.int32), vm((R, O), BF16), vm((T, OUT, O), F32),
        vm((X, 2, R2, O), BF16), vm((Z, 2, 2, R2, O), BF16), vm((Z, 2, 2, 1, R2), F32),
        vm((X, 1, R), F32), vm((T, O, O), BF16), vm((U, 2, R2, O), BF16),
        vm((U, 2 * X, 2, R2, O), BF16), vm((2 * X, R2, R), F32),
        vm((U, 2, X * R, Z * 2 * R), BF16), vm((U + 1, X * R, O), BF16), vm((U, 2, R, O), F32), vm((Q, CH, O), F32),
        vm((Q, X, OUT, O), BF16), vm((Q, X, OUT, O), BF16),
        vm((Q, X - 1, OUT, O), BF16), vm((Q, X - 1, OUT, O), BF16),
        vm((Q, OUT, O), BF16), vm((U, 2, 3, OUT, O), BF16), vm((U, 2, OUT, O), BF16),
        vm((U, 2, X, OUT, O), BF16), vm((U, 2, X, OUT, O), BF16),
        vm((U, OUT, O), BF16), vm((U, OUT, O), BF16), vm((U, 2, OUT, O), F32),
        dma((T,)), dma((4,)), dma((T,)),
        dma((Z, 2, HP)), dma((Z, 2, HP)), dma((Z, HP)), dma((Z, HP)),
        dma((Z, 2, HP)), dma((Z, 2, HP)), dma((Z, 2)), dma((Z, 2)), dma((X,)), dma((X,)),
        dma((X, 2)), dma((X, 2)), dma((U, 2, HP)), dma((U, 2, HP)),
        dma((U, X, 2, HP)), dma((U, X, 2, HP)),
        dma((Q,)), dma((Q,)), dma((Q, X - 1)), dma((Q, X - 1)),
        dma((U, 2, 3)), dma((U, 2, 3)), dma((U, 2)), dma((U, 2)),
        dma((U, 2, X)), dma((U, 2, X)), dma((U,)), dma((U,)),
    ]
    result = pl.pallas_call(
        functools.partial(kernel, (Z, X, HP)),
        out_shape=jax.ShapeDtypeStruct((T, OUT, O), F32),
        in_specs=[pl.BlockSpec(memory_space=pl.ANY)] * 5,
        out_specs=pl.BlockSpec(memory_space=pl.ANY),
        scratch_shapes=scratch,
        compiler_params=pltpu.CompilerParams(
            collective_id=0, has_side_effects=True, vmem_limit_bytes=53 * 2**20),
    )(pattern, factors, coulomb.reshape(1, R), coulomb.reshape(2, 1, R2), green)
    return jnp.transpose(result, (1, 0, 2))


def solution(mesh):
    in_specs = (P("tm", None, None), P("aux", None), P("aux", None), P("aux"))
    out_specs = P("aux", "tm", None)
    return jax.shard_map(local, mesh=mesh, in_specs=in_specs, out_specs=out_specs, check_vma=False)
```

```python
import functools

import jax
import jax.numpy as jnp
from jax import lax
from jax.experimental import pallas as pl
from jax.experimental.pallas import tpu as pltpu
from jax.sharding import PartitionSpec as P

MESH = pl.DeviceIdType.MESH
F32, BF16 = jnp.float32, jnp.bfloat16


def turned(p):
    return p + lax.div(p, 2) * (1 - 2 * lax.rem(p, 2))


def dot(a, b, da, db):
    return lax.dot_general(a, b, (((da,), (db,)), ((), ())), preferred_element_type=F32)


def kernel(cfg, pattern_hbm, factors_hbm, coul_hbm, halves_hbm, green_hbm, out_hbm,
           pattern, factors, out,           pm, rows, weights, pweights, green, psend, lhs, cp, kern, car, sig,
           csend, crecv, xsend, xrecv, zsend, zrecv, nrecv, gsend, grecv, tsend, trecv, fin,
           gsem, isem, osem, z_s, z_r, y_s, y_r, s_s, s_r, w_s, w_r, pw_s, pw_r,
           m_s, m_r, p_s, p_r, f_s, f_r, rc_s, rc_r, rx_s, rx_r, rz_s, rz_r,
           rn_s, rn_r, rg_s, rg_r, rt_s, rt_r):
    Z, X, HP = cfg
    T, O = green.shape[0], green.shape[1]
    U = T // 2
    R2 = pm.shape[2]
    R = 2 * R2
    PR = R2 // HP
    OUT = out.shape[1]
    CH = 2 * X * OUT
    tms = lax.axis_size("tm")
    a, tmi = lax.axis_index("aux"), lax.axis_index("tm")
    c = lax.rem(a, 2)
    x = lax.rem(lax.div(a, 2), X)
    z = lax.div(a, 2 * X)
    pos = turned(z)
    upper = lax.div(tmi, tms // 2)
    partner = lax.rem(tmi + tms // 2, tms)
    plane = lax.rem(tmi, 2)
    mate = tmi + 1 - 2 * plane

    def dev(z_, x_, c_):
        return (z_ * X + x_) * 2 + c_

    def xo(e):
        return lax.rem(x + e, X)

    def zo(f):
        return lax.rem(z + f, Z)

    def ring(k):
        return turned(lax.rem(pos + k, Z))

    sibling = dev(z, x, 1 - c)
    nextd = dev(ring(1), x, c)
    sent = []

    def send(src, dst, s, r, **where):
        copy = pltpu.make_async_remote_copy(
            src_ref=src, dst_ref=dst, send_sem=s, recv_sem=r,
            device_id=where, device_id_type=MESH)
        copy.start()
        sent.append(copy)
        return copy

    def slot(j):
        return (1 - upper) * U + j if j < U else upper * U + j - U

    loads = [pltpu.make_async_copy(green_hbm.at[slot(j)], green.at[j], gsem.at[j]) for j in range(T)]
    barrier = pltpu.get_barrier_semaphore()
    friends = [{"aux": dev(zo(f), x, c)} for f in range(1, Z)]
    friends += [{"aux": dev(zo(f), x, 1 - c)} for f in range(Z)]
    friends += [{"aux": dev(z, xo(e), c)} for e in range(1, X)]
    friends += [{"tm": partner}]
    if tms > 2:
        friends += [{"tm": mate}]
    for where in friends:
        pl.semaphore_signal(barrier, inc=1, device_id=where, device_id_type=MESH)
    plane_rows = [pl.ds(pl.multiple_of(h * R2, R2), R2) for h in (plane, 1 - plane)]
    inputs = [(pattern_hbm, pattern), (factors_hbm.at[plane_rows[0]], factors.at[0]),
              (factors_hbm.at[plane_rows[1]], factors.at[1]), (coul_hbm, pweights.at[0]),
              (halves_hbm, weights.at[0, 0])]
    inputs = [pltpu.make_async_copy(src, dst, isem.at[n]) for n, (src, dst) in enumerate(inputs)]
    for copy in inputs + loads:
        copy.start()

    brows = R // pattern.shape[0]
    bcols = O // pattern.shape[1]
    step = min(brows, R2)

    def mask(n, half):
        inputs[1 + n].wait()
        for r0 in range(0, R2, step):
            for j in range(pattern.shape[1]):
                rs, cs = pl.ds(r0, step), pl.ds(j * bcols, bcols)
                there = pattern[lax.div(half * R2 + r0, brows), j].astype(F32)
                part = (factors[n, rs, cs].astype(F32) * there).astype(BF16)
                pm[0, half, rs, cs] = part
                rows[0, half, 0, rs, cs] = part

    def cut(i):
        return pl.ds(i * PR, PR)

    zc, yc, sc, wc, pwc, mc, pc, fc = {}, {}, {}, {}, {}, {}, {}, {}

    inputs[0].wait()
    mask(0, plane)
    pl.semaphore_wait(barrier, len(friends))
    for i in range(HP):
        zc[1, 0, i] = send(pm.at[0, plane, cut(i)], rows.at[1, plane, 0, cut(i)],
                           z_s.at[1, 0, i], z_r.at[1, 0, i], aux=nextd)
    for n, half in enumerate((plane, 1 - plane)):
        if n:
            mask(n, half)
        for e in range(1, X):
            mc[e, n] = send(pm.at[0, half], pm.at[X - e, half], m_s.at[e, n], m_r.at[e, n],
                            aux=dev(z, xo(e), c))
        sc[0, n, 0] = send(pm.at[0, half], rows.at[0, half, 1], s_s.at[0, n, 0], s_r.at[0, n, 0], aux=sibling)
    inputs[3].wait()
    inputs[4].wait()
    for e in range(1, X):
        pwc[e] = send(pweights.at[0], pweights.at[X - e], pw_s.at[e], pw_r.at[e], aux=dev(z, xo(e), c))
    for k in range(Z):
        for s in range(2):
            if k + s:
                wc[k, s] = send(weights.at[0, 0], weights.at[k, s], w_s.at[k, s], w_r.at[k, s],
                                aux=dev(ring(k), x, c + s * (1 - 2 * c)))

    def project(g, e, turn, store):
        def one(j, carry):
            at = pl.ds(pl.multiple_of(j * 256, 256), 256)
            m = pm[e].reshape(R, O)
            value = dot(m, green[g, at, :], 1, 1) if turn else dot(m, green[g, :, at], 1, 0)
            store(at, value.astype(BF16))
            return carry
        lax.fori_loop(0, O // 256, one, 0)

    def to_partner(u):
        loads[u].wait()

        def store(at, value):
            psend[u, 0, :, at] = value[:R2]
            psend[u, 1, :, at] = value[R2:]
        project(u, 0, True, store)
        for h in range(2):
            for i in range(HP):
                pc[u, h, i] = send(psend.at[u, h, cut(i)], lhs.at[u, h, 1, cut(i)],
                                   p_s.at[u, h, i], p_r.at[u, h, i], tm=partner)

    def keep(u, e):
        def store(at, value):
            lhs[u, 2 * e, 0, :, at] = value[:R2]
            lhs[u, 2 * e + 1, 0, :, at] = value[R2:]
        project(U + u, e, False, store)

    for u in range(U):
        to_partner(u)
    for u in range(U):
        loads[U + u].wait()
        keep(u, 0)

    def half_of(w):
        return plane if w == 0 else 1 - plane

    def across(k, w, i):
        half = half_of(w)
        sc[k, w, i] = send(rows.at[k, half, 0, cut(i)], rows.at[k, half, 1, cut(i)],
                           s_s.at[k, w, i], s_r.at[k, w, i], aux=sibling)

    def forward(k, w, i):
        half = half_of(w)
        zc[k + 1, w, i] = send(rows.at[k, half, 0, cut(i)], rows.at[k + 1, half, 0, cut(i)],
                               z_s.at[k + 1, w, i], z_r.at[k + 1, w, i], aux=nextd)

    def share(k, i):
        yc[k, i] = send(rows.at[k, plane, 0, cut(i)], rows.at[k, plane, 0, cut(i)],
                        y_s.at[k, i], y_r.at[k, i], tm=mate)

    def on_z(k, w, i, share_now=True):
        zc[k, w, i].wait_recv()
        if k < Z - 1:
            forward(k, w, i)
            if share_now:
                share(k, i)
        across(k, w, i)

    def on_y(k, i):
        yc[k, i].wait_recv()
        if k == Z - 2:
            forward(k, 1, i)
        across(k, 1, i)

    def on_p(u, h, i):
        pc[u, h, i].wait_recv()
        for e in range(1, X):
            fc[u, e, h, i] = send(lhs.at[u, h, 1, cut(i)], lhs.at[u, 2 * (X - e) + h, 1, cut(i)],
                                  f_s.at[u, e, h, i], f_r.at[u, e, h, i], aux=dev(z, xo(e), c))

    waited = set()

    def once(*copies):
        for copy in copies:
            if id(copy) not in waited:
                waited.add(id(copy))
                copy.wait_recv()

    def set_cp(e):
        cp[2 * e] = jnp.transpose(jnp.broadcast_to(pweights[e], (R, R)))[:R2]
        cp[2 * e + 1] = jnp.transpose(jnp.broadcast_to(pweights[e], (R, R)))[R2:]

    def others(e):
        for h in range(2):
            once(mc[e, h])
        once(pwc[e])
        set_cp(e)
        for u in range(U):
            keep(u, e)

    def need(k, w):
        if k == 0:
            once(sc[0, 0, 0], sc[0, 1, 0])
        else:
            for i in range(HP):
                once(sc[k, w, i])
        for s in range(2):
            if k + s:
                once(wc[k, s])

    def tiles(p0, pn, k, w):
        need(k, w)
        half = w if k == 0 else half_of(w)
        at = pl.ds(pl.multiple_of((k * 2 + half) * R, R), R)
        g = min(pn, 2)

        def one(n, carry):
            u, p = lax.div(n, pn // g), p0 + g * lax.rem(n, pn // g)
            both = dot(lhs[u, pl.ds(p, g)].reshape(g * R, O), rows[k, half].reshape(R, O), 1, 1)
            wq = jnp.concatenate([weights[k, 0, half], weights[k, 1, half]], axis=1)
            for i in range(g):
                ax, bx = both[i * R:i * R + R2], both[i * R + R2:(i + 1) * R]
                w_ = ax * bx * (cp[p + i] * wq)
                to = pl.ds(pl.multiple_of((p + i) * R2, R2), R2)
                kern[u, 0, to, at] = (w_ * ax).astype(BF16)
                kern[u, 1, to, at] = (w_ * bx).astype(BF16)
            return carry
        lax.fori_loop(0, U * (pn // g), one, 0)

    todo = []

    def plan(when, what, *args):
        todo.append((when, len(todo), what, args))

    def run_plan():
        for _, _, what, args in sorted(todo, key=lambda item: item[:2]):
            what(*args)
        todo.clear()

    PT, L = 5.6 / HP, 1.6
    for i in range(HP):
        plan(PT * (i + 1) + L, on_z, 1, 0, i, False)
        plan(5.6 + PT * (i + 1) + L, on_z, 2, 0, i)
        plan(11.2 + PT * (i + 1) + L, on_z, 3, 0, i)
        plan(16.8 + PT * (i + 1) + L, on_z, 3, 1, i)
        plan(12.8 + PT * (i + 1) + L + 0.1, on_y, 2, i)
        plan(18.4 + PT * (i + 1) + L, on_y, 1, i)
        plan(5.6 + PT * HP + L + 0.05, share, 1, i)
        for h in range(2):
            plan(0.8 + (5.6 * h + PT * (i + 1)) + L + 0.05, lambda h, i: [on_p(u, h, i) for u in range(U)], h, i)
    for e in range(1, X):
        plan(13.0, others, e)
    plan(1.0, set_cp, 0)
    t0 = 13.9
    plan(t0, tiles, 0, 2, 0, 0)
    plan(t0, tiles, 0, 2, 0, 1)
    plan(t0 + 0.3, tiles, 0, 2, 1, 0)
    plan(t0 + 1.5, tiles, 0, 2, 2, 0)
    plan(19.8, tiles, 0, 2, 3, 0)
    plan(20.7, tiles, 0, 2, 2, 1)

    def got(h):
        for u in range(U):
            for e in range(1, X):
                for i in range(HP):
                    once(fc[u, e, h, i])

    def rest(h, units):
        got(h)
        for e in range(1, X):
            for k, w in units:
                tiles(2 * e + h, 1, k, w)
    plan(18.9, rest, 0, [(0, 0), (0, 1), (1, 0), (2, 0)])
    plan(22.7, rest, 0, [(3, 0), (2, 1)])
    early = [(0, 0), (0, 1), (1, 0), (2, 0), (3, 0), (2, 1)]
    plan(24.7, rest, 1, early)
    plan(26.0, tiles, 0, 2 * X, 3, 1)
    plan(26.6, tiles, 0, 2 * X, 1, 1)
    run_plan()

    def column(k, half):
        return pl.ds(pl.multiple_of((k * 2 + half) * R, R), R)

    def carried(u, typ, at, width):
        near = dot(kern[u, typ, pl.ds(0, R)], rows[:, :, :, :, at].reshape(Z * 2 * R, width), 1, 0)
        far = dot(kern[u, typ, pl.ds(R, (X - 1) * R)], rows[:, :, :, :, at].reshape(Z * 2 * R, width), 1, 0)
        return jnp.concatenate([near.astype(BF16), far.astype(BF16)], axis=0)

    def block(u, n):
        width = O // 4
        at = pl.ds(n * width, width)
        car[u, :, at] = carried(u, 0, at, width)

    DIAG, CROSS, NB, OWN = range(4)
    ZF, DIRECT = (1,), ()
    nbz = z + 1 - 2 * lax.rem(z, 2)
    target = [lax.rem(nbz + 2, Z), zo(2), nbz, z]
    nbd, crossd = dev(nbz, x, c), dev(zo(2), x, c)
    cross, xc, nc, gc, zf, tc = {}, {}, {}, {}, {}, {}

    def index(u, typ, d):
        return (u * 2 + typ) * 4 + d

    def stage_a(u, typ, d):
        q = index(u, typ, d)
        base = target[d] * CH
        at = pl.ds(pl.multiple_of(base, CH), CH)
        if typ:
            car[U, :, pl.ds(0, CH)] = carried(u, 1, at, CH)
            sig[q] = dot(car[U, :, pl.ds(0, CH)], pm[...].reshape(X * R, O), 0, 0)
        else:
            sig[q] = dot(pm[:, :, :, at].reshape(X * R, CH), car[u], 0, 0)
        for g in range(X):
            mine = pl.ds(pl.multiple_of((g * 2 + 1 - c) * OUT, OUT), OUT)
            csend[q, g] = sig[q, mine, :].astype(BF16)
        cross[q] = send(csend.at[q], crecv.at[q], rc_s.at[q], rc_r.at[q], aux=sibling)

    def summed(u, typ, d, g):
        q = index(u, typ, d)
        at = pl.ds(pl.multiple_of((g * 2 + c) * OUT, OUT), OUT)
        value = sig[q, at, :] + crecv[q, g].astype(F32)
        if d == OWN and typ in ZF:
            value = value + grecv[u, typ, g].astype(F32)
        return value

    def stage_g(u, typ, part):
        once(cross[index(u, typ, NB)])
        for g in range(X):
            if g * 2 // X == part:
                gsend[u, typ, g] = summed(u, typ, NB, g).astype(BF16)
                gc[u, typ, g] = send(gsend.at[u, typ, g], grecv.at[u, typ, g], rg_s.at[u, typ, g],
                                     rg_r.at[u, typ, g], aux=nbd)

    def stage_b(u, typ, d):
        q = index(u, typ, d)
        once(cross[q])
        if d == OWN and typ in ZF:
            once(*[gc[u, typ, g] for g in range(X)])
        for e in range(1, X):
            xsend[q, e - 1] = summed(u, typ, d, xo(e)).astype(BF16)
            xc[q, e] = send(xsend.at[q, e - 1], xrecv.at[q, e - 1], rx_s.at[q, e - 1],
                            rx_r.at[q, e - 1], aux=dev(z, xo(e), c))

    def stage_c(u, typ, d):
        q = index(u, typ, d)
        for e in range(1, X):
            once(xc[q, e])
        value = summed(u, typ, d, x)
        for e in range(1, X):
            value = value + xrecv[q, e - 1].astype(F32)
        if d == CROSS and typ not in DIRECT:
            once(nc[u, typ])
            value = value + nrecv[u, typ].astype(F32)
        if d == OWN:
            fin[u, typ] = value
            return
        zsend[q] = value.astype(BF16)
        if d == DIAG and typ in DIRECT:
            zf[u, typ, 2] = send(zsend.at[q], zrecv.at[u, typ, 2], rz_s.at[u, typ, 2],
                                 rz_r.at[u, typ, 2], aux=dev(target[DIAG], x, c))
        elif d == DIAG:
            nc[u, typ] = send(zsend.at[q], nrecv.at[u, typ], rn_s.at[u, typ], rn_r.at[u, typ], aux=nbd)
        else:
            to = 0 if d == NB else 1
            zf[u, typ, to] = send(zsend.at[q], zrecv.at[u, typ, to], rz_s.at[u, typ, to],
                                  rz_r.at[u, typ, to], aux=nbd if d == NB else crossd)

    ends = []

    def finish(n, t):
        copy = pltpu.make_async_copy(out.at[t], out_hbm.at[t], osem.at[n])
        copy.start()
        ends.append(copy)

    def stage_d(u, typ):
        value = fin[u, typ]
        for to in (2, 1, 0):
            if (to == 0 and typ not in ZF) or to == 1 or (to == 2 and typ in DIRECT):
                once(zf[u, typ, to])
                value = value + zrecv[u, typ, to].astype(F32)
        if typ:
            tsend[u] = value.astype(BF16)
            tc[u] = send(tsend.at[u], trecv.at[u], rt_s.at[u], rt_r.at[u], tm=partner)
        else:
            out[upper * U + u] = value
            finish(u, upper * U + u)

    def stage_e(u):
        once(tc[u])
        out[(1 - upper) * U + u] = trecv[u].astype(F32)
        finish(U + u, (1 - upper) * U + u)

    steps = (
        ("A", 1, DIAG), ("A", 1, NB), ("B", 1, DIAG), ("A", 1, CROSS), ("G", 1, 0), ("W", 0),
        ("B", 1, CROSS), ("W", 1), ("W", 2), ("W", 3), ("A", 0, DIAG), ("C", 1, DIAG),
        ("G", 1, 1), ("A", 0, CROSS), ("B", 0, DIAG), ("B", 0, CROSS), ("A", 1, OWN), ("A", 0, NB),
        ("C", 1, CROSS), ("B", 0, NB), ("A", 0, OWN), ("B", 1, OWN), ("C", 0, DIAG), ("C", 0, CROSS),
        ("B", 0, OWN), ("C", 0, NB), ("C", 1, OWN), ("D", 1), ("C", 0, OWN), ("E",),
        ("D", 0),
    )
    run = {"A": stage_a, "B": stage_b, "C": stage_c, "D": stage_d, "E": stage_e, "G": stage_g, "W": block}
    for u in range(U):
        for step in steps:
            run[step[0]](u, *step[1:])
    for copy in sent:
        copy.wait_send()
    for copy in ends:
        copy.wait()


def local(green, factors, pattern, coulomb):
    n = lax.axis_size("aux")
    T, O, _ = green.shape
    R = factors.shape[0]
    chips = n // 2
    Z = 4
    X = chips // Z
    HP = 2
    R2 = R // 2
    U = T // 2
    OUT = O // n
    CH = 2 * X * OUT
    Q = U * 2 * Z
    dma = pltpu.SemaphoreType.DMA
    vm = pltpu.VMEM
    scratch = [
        pltpu.SMEM(pattern.shape, jnp.int32), vm((2, R2, O), BF16), vm((T, OUT, O), F32),
        vm((X, 2, R2, O), BF16), vm((Z, 2, 2, R2, O), BF16), vm((Z, 2, 2, 1, R2), F32),
        vm((X, 1, R), F32), vm((T, O, O), BF16), vm((U, 2, R2, O), BF16),
        vm((U, 2 * X, 2, R2, O), BF16), vm((2 * X, R2, R), F32),
        vm((U, 2, X * R, Z * 2 * R), BF16), vm((U + 1, X * R, O), BF16), vm((Q, CH, O), F32),
        vm((Q, X, OUT, O), BF16), vm((Q, X, OUT, O), BF16),
        vm((Q, X - 1, OUT, O), BF16), vm((Q, X - 1, OUT, O), BF16),
        vm((Q, OUT, O), BF16), vm((U, 2, 3, OUT, O), BF16), vm((U, 2, OUT, O), BF16),
        vm((U, 2, X, OUT, O), BF16), vm((U, 2, X, OUT, O), BF16),
        vm((U, OUT, O), BF16), vm((U, OUT, O), BF16), vm((U, 2, OUT, O), F32),
        dma((T,)), dma((5,)), dma((T,)),
        dma((Z, 2, HP)), dma((Z, 2, HP)), dma((Z, HP)), dma((Z, HP)),
        dma((Z, 2, HP)), dma((Z, 2, HP)), dma((Z, 2)), dma((Z, 2)), dma((X,)), dma((X,)),
        dma((X, 2)), dma((X, 2)), dma((U, 2, HP)), dma((U, 2, HP)),
        dma((U, X, 2, HP)), dma((U, X, 2, HP)),
        dma((Q,)), dma((Q,)), dma((Q, X - 1)), dma((Q, X - 1)),
        dma((U, 2, 3)), dma((U, 2, 3)), dma((U, 2)), dma((U, 2)),
        dma((U, 2, X)), dma((U, 2, X)), dma((U,)), dma((U,)),
    ]
    result = pl.pallas_call(
        functools.partial(kernel, (Z, X, HP)),
        out_shape=jax.ShapeDtypeStruct((T, OUT, O), F32),
        in_specs=[pl.BlockSpec(memory_space=pl.ANY)] * 5,
        out_specs=pl.BlockSpec(memory_space=pl.ANY),
        scratch_shapes=scratch,
        compiler_params=pltpu.CompilerParams(
            collective_id=0, has_side_effects=True, vmem_limit_bytes=53 * 2**20),
    )(pattern, factors, coulomb.reshape(1, R), coulomb.reshape(2, 1, R2), green)
    return jnp.transpose(result, (1, 0, 2))


def solution(mesh):
    in_specs = (P("tm", None, None), P("aux", None), P("aux", None), P("aux"))
    out_specs = P("aux", "tm", None)
    return jax.shard_map(local, mesh=mesh, in_specs=in_specs, out_specs=out_specs, check_vma=False)
```

```python
import functools

import jax
import jax.numpy as jnp
from jax import lax
from jax.experimental import pallas as pl
from jax.experimental.pallas import tpu as pltpu
from jax.sharding import PartitionSpec as P

MESH = pl.DeviceIdType.MESH
F32, BF16 = jnp.float32, jnp.bfloat16


def turned(p):
    return p + lax.div(p, 2) * (1 - 2 * lax.rem(p, 2))


def dot(a, b, da, db):
    return lax.dot_general(a, b, (((da,), (db,)), ((), ())), preferred_element_type=F32)


def kernel(cfg, pattern_hbm, factors_hbm, coul_hbm, halves_hbm, green_hbm, out_hbm,
           pattern, factors, out,           pm, rows, weights, pweights, green, psend, lhs, cp, kern, car, sig,
           csend, crecv, xsend, xrecv, zsend, zrecv, nrecv, gsend, grecv, tsend, trecv, fin,
           gsem, isem, osem, z_s, z_r, y_s, y_r, s_s, s_r, w_s, w_r, pw_s, pw_r,
           m_s, m_r, p_s, p_r, f_s, f_r, rc_s, rc_r, rx_s, rx_r, rz_s, rz_r,
           rn_s, rn_r, rg_s, rg_r, rt_s, rt_r):
    Z, X, HP = cfg
    T, O = green.shape[0], green.shape[1]
    U = T // 2
    R2 = pm.shape[2]
    R = 2 * R2
    PR = R2 // HP
    OUT = out.shape[1]
    CH = 2 * X * OUT
    tms = lax.axis_size("tm")
    a, tmi = lax.axis_index("aux"), lax.axis_index("tm")
    c = lax.rem(a, 2)
    x = lax.rem(lax.div(a, 2), X)
    z = lax.div(a, 2 * X)
    pos = turned(z)
    upper = lax.div(tmi, tms // 2)
    partner = lax.rem(tmi + tms // 2, tms)
    plane = lax.rem(tmi, 2)
    mate = tmi + 1 - 2 * plane

    def dev(z_, x_, c_):
        return (z_ * X + x_) * 2 + c_

    def xo(e):
        return lax.rem(x + e, X)

    def zo(f):
        return lax.rem(z + f, Z)

    def ring(k):
        return turned(lax.rem(pos + k, Z))

    sibling = dev(z, x, 1 - c)
    nextd = dev(ring(1), x, c)
    sent = []

    def send(src, dst, s, r, **where):
        copy = pltpu.make_async_remote_copy(
            src_ref=src, dst_ref=dst, send_sem=s, recv_sem=r,
            device_id=where, device_id_type=MESH)
        copy.start()
        sent.append(copy)
        return copy

    def slot(j):
        return (1 - upper) * U + j if j < U else upper * U + j - U

    loads = [pltpu.make_async_copy(green_hbm.at[slot(j)], green.at[j], gsem.at[j]) for j in range(T)]
    barrier = pltpu.get_barrier_semaphore()
    friends = [{"aux": dev(zo(f), x, c)} for f in range(1, Z)]
    friends += [{"aux": dev(zo(f), x, 1 - c)} for f in range(Z)]
    friends += [{"aux": dev(z, xo(e), c)} for e in range(1, X)]
    friends += [{"tm": partner}]
    if tms > 2:
        friends += [{"tm": mate}]
    for where in friends:
        pl.semaphore_signal(barrier, inc=1, device_id=where, device_id_type=MESH)
    plane_rows = [pl.ds(pl.multiple_of(h * R2, R2), R2) for h in (plane, 1 - plane)]
    inputs = [(pattern_hbm, pattern), (factors_hbm.at[plane_rows[0]], factors.at[0]),
              (factors_hbm.at[plane_rows[1]], factors.at[1]), (coul_hbm, pweights.at[0]),
              (halves_hbm, weights.at[0, 0])]
    inputs = [pltpu.make_async_copy(src, dst, isem.at[n]) for n, (src, dst) in enumerate(inputs)]
    for copy in inputs + loads:
        copy.start()

    brows = R // pattern.shape[0]
    bcols = O // pattern.shape[1]
    step = min(brows, R2)

    def mask(n, half):
        inputs[1 + n].wait()
        for r0 in range(0, R2, step):
            for j in range(pattern.shape[1]):
                rs, cs = pl.ds(r0, step), pl.ds(j * bcols, bcols)
                there = pattern[lax.div(half * R2 + r0, brows), j].astype(F32)
                part = (factors[n, rs, cs].astype(F32) * there).astype(BF16)
                pm[0, half, rs, cs] = part
                rows[0, half, 0, rs, cs] = part

    def cut(i):
        return pl.ds(i * PR, PR)

    zc, yc, sc, wc, pwc, mc, pc, fc = {}, {}, {}, {}, {}, {}, {}, {}

    inputs[0].wait()
    mask(0, plane)
    pl.semaphore_wait(barrier, len(friends))
    for i in range(HP):
        zc[1, 0, i] = send(pm.at[0, plane, cut(i)], rows.at[1, plane, 0, cut(i)],
                           z_s.at[1, 0, i], z_r.at[1, 0, i], aux=nextd)
    for n, half in enumerate((plane, 1 - plane)):
        if n:
            mask(n, half)
        for e in range(1, X):
            mc[e, n] = send(pm.at[0, half], pm.at[X - e, half], m_s.at[e, n], m_r.at[e, n],
                            aux=dev(z, xo(e), c))
        sc[0, n, 0] = send(pm.at[0, half], rows.at[0, half, 1], s_s.at[0, n, 0], s_r.at[0, n, 0], aux=sibling)
    inputs[3].wait()
    inputs[4].wait()
    for e in range(1, X):
        pwc[e] = send(pweights.at[0], pweights.at[X - e], pw_s.at[e], pw_r.at[e], aux=dev(z, xo(e), c))
    for k in range(Z):
        for s in range(2):
            if k + s:
                wc[k, s] = send(weights.at[0, 0], weights.at[k, s], w_s.at[k, s], w_r.at[k, s],
                                aux=dev(ring(k), x, c + s * (1 - 2 * c)))

    def project(g, e, turn, store):
        def one(j, carry):
            at = pl.ds(pl.multiple_of(j * 256, 256), 256)
            m = pm[e].reshape(R, O)
            value = dot(m, green[g, at, :], 1, 1) if turn else dot(m, green[g, :, at], 1, 0)
            store(at, value.astype(BF16))
            return carry
        lax.fori_loop(0, O // 256, one, 0)

    def to_partner(u):
        loads[u].wait()

        def store(at, value):
            psend[u, 0, :, at] = value[:R2]
            psend[u, 1, :, at] = value[R2:]
        project(u, 0, True, store)
        for h in range(2):
            for i in range(HP):
                pc[u, h, i] = send(psend.at[u, h, cut(i)], lhs.at[u, h, 1, cut(i)],
                                   p_s.at[u, h, i], p_r.at[u, h, i], tm=partner)

    def keep(u, e):
        def store(at, value):
            lhs[u, 2 * e, 0, :, at] = value[:R2]
            lhs[u, 2 * e + 1, 0, :, at] = value[R2:]
        project(U + u, e, False, store)

    for u in range(U):
        to_partner(u)
    for u in range(U):
        loads[U + u].wait()
        keep(u, 0)

    def half_of(w):
        return plane if w == 0 else 1 - plane

    def across(k, w, i):
        half = half_of(w)
        sc[k, w, i] = send(rows.at[k, half, 0, cut(i)], rows.at[k, half, 1, cut(i)],
                           s_s.at[k, w, i], s_r.at[k, w, i], aux=sibling)

    def forward(k, w, i):
        half = half_of(w)
        zc[k + 1, w, i] = send(rows.at[k, half, 0, cut(i)], rows.at[k + 1, half, 0, cut(i)],
                               z_s.at[k + 1, w, i], z_r.at[k + 1, w, i], aux=nextd)

    def share(k, i):
        yc[k, i] = send(rows.at[k, plane, 0, cut(i)], rows.at[k, plane, 0, cut(i)],
                        y_s.at[k, i], y_r.at[k, i], tm=mate)

    def on_z(k, w, i, share_now=True):
        zc[k, w, i].wait_recv()
        if k < Z - 1:
            forward(k, w, i)
            if share_now:
                share(k, i)
        across(k, w, i)

    def on_y(k, i):
        yc[k, i].wait_recv()
        if k == Z - 2:
            forward(k, 1, i)
        across(k, 1, i)

    def on_p(u, h, i):
        pc[u, h, i].wait_recv()
        for e in range(1, X):
            fc[u, e, h, i] = send(lhs.at[u, h, 1, cut(i)], lhs.at[u, 2 * (X - e) + h, 1, cut(i)],
                                  f_s.at[u, e, h, i], f_r.at[u, e, h, i], aux=dev(z, xo(e), c))

    waited = set()

    def once(*copies):
        for copy in copies:
            if id(copy) not in waited:
                waited.add(id(copy))
                copy.wait_recv()

    def set_cp(e):
        cp[2 * e] = jnp.transpose(jnp.broadcast_to(pweights[e], (R, R)))[:R2]
        cp[2 * e + 1] = jnp.transpose(jnp.broadcast_to(pweights[e], (R, R)))[R2:]

    def others(e):
        for h in range(2):
            once(mc[e, h])
        once(pwc[e])
        set_cp(e)
        for u in range(U):
            keep(u, e)

    def need(k, w):
        if k == 0:
            once(sc[0, 0, 0], sc[0, 1, 0])
        else:
            for i in range(HP):
                once(sc[k, w, i])
        for s in range(2):
            if k + s:
                once(wc[k, s])

    def tiles(p0, pn, k, w):
        need(k, w)
        half = w if k == 0 else half_of(w)
        at = pl.ds(pl.multiple_of((k * 2 + half) * R, R), R)
        g = min(pn, 2)

        def one(n, carry):
            u, p = lax.div(n, pn // g), p0 + g * lax.rem(n, pn // g)
            both = dot(lhs[u, pl.ds(p, g)].reshape(g * R, O), rows[k, half].reshape(R, O), 1, 1)
            wq = jnp.concatenate([weights[k, 0, half], weights[k, 1, half]], axis=1)
            for i in range(g):
                ax, bx = both[i * R:i * R + R2], both[i * R + R2:(i + 1) * R]
                w_ = ax * bx * (cp[p + i] * wq)
                to = pl.ds(pl.multiple_of((p + i) * R2, R2), R2)
                kern[u, 0, to, at] = (w_ * ax).astype(BF16)
                kern[u, 1, to, at] = (w_ * bx).astype(BF16)
            return carry
        lax.fori_loop(0, U * (pn // g), one, 0)

    todo = []

    def plan(when, what, *args):
        todo.append((when, len(todo), what, args))

    def run_plan():
        for _, _, what, args in sorted(todo, key=lambda item: item[:2]):
            what(*args)
        todo.clear()

    PT, L = 5.6 / HP, 1.6
    for i in range(HP):
        plan(PT * (i + 1) + L, on_z, 1, 0, i, False)
        plan(5.6 + PT * (i + 1) + L, on_z, 2, 0, i)
        plan(11.2 + PT * (i + 1) + L, on_z, 3, 0, i)
        plan(16.8 + PT * (i + 1) + L, on_z, 3, 1, i)
        plan(12.8 + PT * (i + 1) + L + 0.1, on_y, 2, i)
        plan(18.4 + PT * (i + 1) + L, on_y, 1, i)
        plan(5.6 + PT * HP + L + 0.05, share, 1, i)
        for h in range(2):
            plan(0.8 + (5.6 * h + PT * (i + 1)) + L + 0.05, lambda h, i: [on_p(u, h, i) for u in range(U)], h, i)
    for e in range(1, X):
        plan(13.0, others, e)
    plan(1.0, set_cp, 0)
    t0 = 13.9
    plan(t0, tiles, 0, 2, 0, 0)
    plan(t0, tiles, 0, 2, 0, 1)
    plan(t0 + 0.3, tiles, 0, 2, 1, 0)
    plan(t0 + 1.5, tiles, 0, 2, 2, 0)
    plan(19.8, tiles, 0, 2, 3, 0)
    plan(20.7, tiles, 0, 2, 2, 1)

    def got(h):
        for u in range(U):
            for e in range(1, X):
                for i in range(HP):
                    once(fc[u, e, h, i])

    def rest(h, units):
        got(h)
        for e in range(1, X):
            for k, w in units:
                tiles(2 * e + h, 1, k, w)
    plan(18.9, rest, 0, [(0, 0), (0, 1), (1, 0), (2, 0)])
    plan(22.7, rest, 0, [(3, 0), (2, 1)])
    early = [(0, 0), (0, 1), (1, 0), (2, 0), (3, 0), (2, 1)]
    plan(24.7, rest, 1, early)
    plan(26.0, tiles, 0, 2 * X, 3, 1)
    plan(26.6, tiles, 0, 2 * X, 1, 1)
    run_plan()

    def column(k, half):
        return pl.ds(pl.multiple_of((k * 2 + half) * R, R), R)

    def carried(u, typ, at, width):
        near = dot(kern[u, typ, pl.ds(0, R)], rows[:, :, :, :, at].reshape(Z * 2 * R, width), 1, 0)
        far = dot(kern[u, typ, pl.ds(R, (X - 1) * R)], rows[:, :, :, :, at].reshape(Z * 2 * R, width), 1, 0)
        return jnp.concatenate([near.astype(BF16), far.astype(BF16)], axis=0)

    def block(u, n):
        width = O // 4
        at = pl.ds(n * width, width)
        car[u, :, at] = carried(u, 0, at, width)

    DIAG, CROSS, NB, OWN = range(4)
    ZF, DIRECT = (1,), ()
    nbz = z + 1 - 2 * lax.rem(z, 2)
    target = [lax.rem(nbz + 2, Z), zo(2), nbz, z]
    nbd, crossd = dev(nbz, x, c), dev(zo(2), x, c)
    cross, xc, nc, gc, zf, tc = {}, {}, {}, {}, {}, {}

    def index(u, typ, d):
        return (u * 2 + typ) * 4 + d

    def stage_a(u, typ, d):
        q = index(u, typ, d)
        base = target[d] * CH
        at = pl.ds(pl.multiple_of(base, CH), CH)
        if typ:
            car[U, :, pl.ds(0, CH)] = carried(u, 1, at, CH)
            sig[q] = dot(car[U, :, pl.ds(0, CH)], pm[...].reshape(X * R, O), 0, 0)
        else:
            sig[q] = dot(pm[:, :, :, at].reshape(X * R, CH), car[u], 0, 0)
        for g in range(X):
            mine = pl.ds(pl.multiple_of((g * 2 + 1 - c) * OUT, OUT), OUT)
            csend[q, g] = sig[q, mine, :].astype(BF16)
        cross[q] = send(csend.at[q], crecv.at[q], rc_s.at[q], rc_r.at[q], aux=sibling)

    def summed(u, typ, d, g):
        q = index(u, typ, d)
        at = pl.ds(pl.multiple_of((g * 2 + c) * OUT, OUT), OUT)
        value = sig[q, at, :] + crecv[q, g].astype(F32)
        if d == OWN and typ in ZF:
            value = value + grecv[u, typ, g].astype(F32)
        return value

    def stage_g(u, typ, part):
        once(cross[index(u, typ, NB)])
        for g in range(X):
            if g * 2 // X == part:
                gsend[u, typ, g] = summed(u, typ, NB, g).astype(BF16)
                gc[u, typ, g] = send(gsend.at[u, typ, g], grecv.at[u, typ, g], rg_s.at[u, typ, g],
                                     rg_r.at[u, typ, g], aux=nbd)

    def stage_b(u, typ, d):
        q = index(u, typ, d)
        once(cross[q])
        if d == OWN and typ in ZF:
            once(*[gc[u, typ, g] for g in range(X)])
        for e in range(1, X):
            xsend[q, e - 1] = summed(u, typ, d, xo(e)).astype(BF16)
            xc[q, e] = send(xsend.at[q, e - 1], xrecv.at[q, e - 1], rx_s.at[q, e - 1],
                            rx_r.at[q, e - 1], aux=dev(z, xo(e), c))

    def stage_c(u, typ, d):
        q = index(u, typ, d)
        for e in range(1, X):
            once(xc[q, e])
        value = summed(u, typ, d, x)
        for e in range(1, X):
            value = value + xrecv[q, e - 1].astype(F32)
        if d == CROSS and typ not in DIRECT:
            once(nc[u, typ])
            value = value + nrecv[u, typ].astype(F32)
        if d == OWN:
            fin[u, typ] = value
            return
        zsend[q] = value.astype(BF16)
        if d == DIAG and typ in DIRECT:
            zf[u, typ, 2] = send(zsend.at[q], zrecv.at[u, typ, 2], rz_s.at[u, typ, 2],
                                 rz_r.at[u, typ, 2], aux=dev(target[DIAG], x, c))
        elif d == DIAG:
            nc[u, typ] = send(zsend.at[q], nrecv.at[u, typ], rn_s.at[u, typ], rn_r.at[u, typ], aux=nbd)
        else:
            to = 0 if d == NB else 1
            zf[u, typ, to] = send(zsend.at[q], zrecv.at[u, typ, to], rz_s.at[u, typ, to],
                                  rz_r.at[u, typ, to], aux=nbd if d == NB else crossd)

    ends = []

    def finish(n, t):
        copy = pltpu.make_async_copy(out.at[t], out_hbm.at[t], osem.at[n])
        copy.start()
        ends.append(copy)

    def stage_d(u, typ):
        value = fin[u, typ]
        for to in (2, 1, 0):
            if (to == 0 and typ not in ZF) or to == 1 or (to == 2 and typ in DIRECT):
                once(zf[u, typ, to])
                value = value + zrecv[u, typ, to].astype(F32)
        if typ:
            tsend[u] = value.astype(BF16)
            tc[u] = send(tsend.at[u], trecv.at[u], rt_s.at[u], rt_r.at[u], tm=partner)
        else:
            out[upper * U + u] = value
            finish(u, upper * U + u)

    def stage_e(u):
        once(tc[u])
        out[(1 - upper) * U + u] = trecv[u].astype(F32)
        finish(U + u, (1 - upper) * U + u)

    steps = (
        ("A", 1, DIAG), ("A", 1, NB), ("B", 1, DIAG), ("A", 1, CROSS), ("G", 1, 0), ("W", 0),
        ("B", 1, CROSS), ("W", 1), ("W", 2), ("W", 3), ("A", 0, DIAG), ("C", 1, DIAG),
        ("G", 1, 1), ("A", 0, CROSS), ("B", 0, DIAG), ("B", 0, CROSS), ("A", 1, OWN), ("A", 0, NB),
        ("B", 0, NB), ("C", 1, CROSS), ("C", 0, DIAG), ("A", 0, OWN), ("B", 1, OWN), ("C", 0, CROSS),
        ("B", 0, OWN), ("C", 0, NB), ("C", 1, OWN), ("D", 1), ("C", 0, OWN), ("E",),
        ("D", 0),
    )
    run = {"A": stage_a, "B": stage_b, "C": stage_c, "D": stage_d, "E": stage_e, "G": stage_g, "W": block}
    for u in range(U):
        for step in steps:
            run[step[0]](u, *step[1:])
    for copy in sent:
        copy.wait_send()
    for copy in ends:
        copy.wait()


def local(green, factors, pattern, coulomb):
    n = lax.axis_size("aux")
    T, O, _ = green.shape
    R = factors.shape[0]
    chips = n // 2
    Z = 4
    X = chips // Z
    HP = 2
    R2 = R // 2
    U = T // 2
    OUT = O // n
    CH = 2 * X * OUT
    Q = U * 2 * Z
    dma = pltpu.SemaphoreType.DMA
    vm = pltpu.VMEM
    scratch = [
        pltpu.SMEM(pattern.shape, jnp.int32), vm((2, R2, O), BF16), vm((T, OUT, O), F32),
        vm((X, 2, R2, O), BF16), vm((Z, 2, 2, R2, O), BF16), vm((Z, 2, 2, 1, R2), F32),
        vm((X, 1, R), F32), vm((T, O, O), BF16), vm((U, 2, R2, O), BF16),
        vm((U, 2 * X, 2, R2, O), BF16), vm((2 * X, R2, R), F32),
        vm((U, 2, X * R, Z * 2 * R), BF16), vm((U + 1, X * R, O), BF16), vm((Q, CH, O), F32),
        vm((Q, X, OUT, O), BF16), vm((Q, X, OUT, O), BF16),
        vm((Q, X - 1, OUT, O), BF16), vm((Q, X - 1, OUT, O), BF16),
        vm((Q, OUT, O), BF16), vm((U, 2, 3, OUT, O), BF16), vm((U, 2, OUT, O), BF16),
        vm((U, 2, X, OUT, O), BF16), vm((U, 2, X, OUT, O), BF16),
        vm((U, OUT, O), BF16), vm((U, OUT, O), BF16), vm((U, 2, OUT, O), F32),
        dma((T,)), dma((5,)), dma((T,)),
        dma((Z, 2, HP)), dma((Z, 2, HP)), dma((Z, HP)), dma((Z, HP)),
        dma((Z, 2, HP)), dma((Z, 2, HP)), dma((Z, 2)), dma((Z, 2)), dma((X,)), dma((X,)),
        dma((X, 2)), dma((X, 2)), dma((U, 2, HP)), dma((U, 2, HP)),
        dma((U, X, 2, HP)), dma((U, X, 2, HP)),
        dma((Q,)), dma((Q,)), dma((Q, X - 1)), dma((Q, X - 1)),
        dma((U, 2, 3)), dma((U, 2, 3)), dma((U, 2)), dma((U, 2)),
        dma((U, 2, X)), dma((U, 2, X)), dma((U,)), dma((U,)),
    ]
    result = pl.pallas_call(
        functools.partial(kernel, (Z, X, HP)),
        out_shape=jax.ShapeDtypeStruct((T, OUT, O), F32),
        in_specs=[pl.BlockSpec(memory_space=pl.ANY)] * 5,
        out_specs=pl.BlockSpec(memory_space=pl.ANY),
        scratch_shapes=scratch,
        compiler_params=pltpu.CompilerParams(
            collective_id=0, has_side_effects=True, vmem_limit_bytes=53 * 2**20),
    )(pattern, factors, coulomb.reshape(1, R), coulomb.reshape(2, 1, R2), green)
    return jnp.transpose(result, (1, 0, 2))


def solution(mesh):
    in_specs = (P("tm", None, None), P("aux", None), P("aux", None), P("aux"))
    out_specs = P("aux", "tm", None)
    return jax.shard_map(local, mesh=mesh, in_specs=in_specs, out_specs=out_specs, check_vma=False)
```
